32 devices in a mesh: dp: 4 (over y, x), seq: 8 (over z, core).
Axes of the slice: x: 2, y: 2, z: 4, core: 2. Of those that a mesh axis runs over, the one named last changes fastest.
Arguments:
- tokens: bfloat16 [4, 1024, 2048], P('dp', 'seq'), may hold values from -6 to 6
- lengths: int32 [4], P('dp'), may hold values from 1024 to 1024, as said below
- w_qkv: bfloat16 [2048, 3072], P('seq', 'dp'), may hold values from -0.5 to 0.5
- w_out: bfloat16 [2048, 2048], P('seq', 'dp'), may hold values from -1 to 1
- w_gate_up: bfloat16 [2048, 16384], P('seq', 'dp'), may hold values from -0.125 to 0.125
- w_down: bfloat16 [8192, 2048], P('seq', 'dp'), may hold values from -0.5 to 0.5
- gains: bfloat16 [2048, 2], P('seq'), may hold values from 0.5 to 1.5
- cotangent: bfloat16 [4, 1024, 2048], P('dp', 'seq'), may hold values from -6 to 6
Outputs:
- output: bfloat16 [4, 1024, 2048], P('dp', 'seq')
- grad_tokens: float32 [4, 1024, 2048], P('dp', 'seq')
- grad_qkv: float32 [2048, 3072], P('seq', 'dp')
- grad_out: float32 [2048, 2048], P('seq', 'dp')
- grad_gate_up: float32 [2048, 16384], P('seq', 'dp')
- grad_down: float32 [8192, 2048], P('seq', 'dp')
- grad_gains: float32 [2048, 2], P('seq')
The draws below stay inside these ranges and needn't reach their ends.
Inputs may be any that keep to these rules, and one draw needn't show every extreme that they name: `lengths`: some sequence uses all 1024 slots.
All inputs are finite; a program needn't handle non-finite values.
Results may differ from the reference program's by a relative error of at most 0.015.
The reference program's roundings to bfloat16 on the way count: a program that leaves them out, or rounds other values in their place, can miss the bound.
Values may be sent and summed in bfloat16 or wider, within the bound.
No kernel may reach another device: no remote copies, remote signals or barrier semaphores. Data moves between devices by JAX's collectives and lax.ppermute only.
A program may use at most 512 MiB of HBM per device.

```python
import math
import jax
import jax.numpy as jnp
from jax import lax

D = 2048
HEADS = 32
KV_HEADS = 8
HEAD_DIM = 64
FF = 8192
MIN_LEN = 1024
SLOTS = 1024
SEQS = 4
ATTN = 2048
QKV = 3072


def draw_lengths(key, part):
    first_key, second_key = jax.random.split(jax.random.fold_in(key, 11))
    drawn = jax.random.randint(first_key, (SEQS,), MIN_LEN, SLOTS + 1)
    fullest = jax.random.randint(second_key, (), 0, SEQS)
    return jnp.where(jnp.arange(SEQS) == fullest, SLOTS, drawn).astype(jnp.int32)


def level_of(key, extent, shards, smallest, top_value):
    loudness, own = 1.0, jax.random.fold_in(key, 6)
    for dim, parts in shards:
        draws = jnp.exp(jax.random.uniform(jax.random.fold_in(own, dim), (parts,), jnp.float32, smallest / len(shards), top_value / len(shards)))
        loudness = loudness * jnp.repeat(draws, extent[dim] // parts).reshape([-1 if axis == dim else 1 for axis in range(len(extent))])
    return loudness


def centred(own_key, shape, deviation, limit, pieces=(), held_as=jnp.bfloat16):
    values = deviation * jax.random.normal(own_key, shape, jnp.float32)
    if pieces:
        values = values * level_of(own_key, shape, pieces, -0.22, 0.18)
    return jnp.clip(values, -limit, limit).astype(held_as)


def setup_inputs(seed: int = 0) -> dict:
    key_of = jax.random.split(jax.random.key(seed), 9)
    tokens = centred(key_of[0], (SEQS, SLOTS, D), 1.0, 6.0, ((0, 4), (1, 8)))
    lengths = draw_lengths(jax.random.fold_in(key_of[8], 71), 0)
    w_qkv = centred(key_of[2], (D, QKV), 128 ** -0.5, 0.5, ((0, 8), (1, 4)))
    w_out = centred(key_of[3], (ATTN, D), 32 ** -0.5, 1.0, ((0, 8), (1, 4)))
    w_gate_up = centred(key_of[4], (D, 2 * FF), D ** -0.5, 0.125, ((0, 8), (1, 4)))
    w_down = centred(key_of[5], (FF, D), 128 ** -0.5, 0.5, ((0, 8), (1, 4)))
    gains = jnp.clip(1.0 + 0.1 * jax.random.normal(key_of[6], (D, 2), jnp.float32), 0.5, 1.5).astype(jnp.bfloat16)
    cotangent = centred(key_of[7], (SEQS, SLOTS, D), 1.0, 6.0, ((0, 4), (1, 8)))
    return dict(tokens=tokens, lengths=lengths, w_qkv=w_qkv, w_out=w_out, w_gate_up=w_gate_up, w_down=w_down, gains=gains, cotangent=cotangent)


EPSILON = 1e-05
RESIDUAL_SCALE = 0.22
SCORE_SCALE = 1.0 / 64.0
ROPE_THETA = 10000000.0
PRECISE = lax.Precision.HIGHEST

@jax.custom_vjp
def low(v):
    return lax.optimization_barrier(v.astype(jnp.bfloat16)).astype(jnp.float32)

@jax.custom_vjp
def low_back(v):
    return v

def low_keep(v):
    return (low(v), None)

def low_pass(kept, grad):
    return (grad,)

def back_keep(v):
    return (v, None)

def back_low(kept, grad):
    return (low(grad),)
low.defvjp(low_keep, low_pass)
low_back.defvjp(back_keep, back_low)

def matmul(left, right):
    return jnp.dot(left, right, precision=PRECISE, preferred_element_type=jnp.float32)

def rms_norm(values, gain):
    inverse = lax.rsqrt(lax.optimization_barrier(jnp.mean(values * values, axis=-1, keepdims=True)) + EPSILON)
    return values * inverse * gain

def rotary(positions):
    half_dim = HEAD_DIM // 2
    frequency = ROPE_THETA ** (-(jnp.arange(half_dim, dtype=jnp.float32) * 2.0) / HEAD_DIM)
    angles = positions.astype(jnp.float32)[:, None] * frequency[None, :]
    angles = jnp.concatenate([angles, angles], axis=1)
    return (jnp.cos(angles), jnp.sin(angles))

def rotate(values, cosine, sine_table):
    half_dim = values.shape[-1] // 2
    turned = jnp.concatenate([-values[..., half_dim:], values[..., :half_dim]], axis=-1)
    return values * cosine[:, None, :] + turned * sine_table[:, None, :]

def layer(seq_tokens, w_qkv, w_out, w_gate_up, w_down, gains, length):
    attn_width = HEADS * HEAD_DIM
    kv_width = KV_HEADS * HEAD_DIM
    group_size = HEADS // KV_HEADS
    block_rows = math.gcd(SLOTS, 512)
    block_count = SLOTS // block_rows
    positions = jnp.arange(SLOTS, dtype=jnp.int32)
    valid_rows = (positions < length).astype(jnp.float32)[:, None]
    cosine, sine_table = rotary(positions)
    normed = low(rms_norm(seq_tokens, gains[:, 0]))
    qkv = low_back(matmul(normed, w_qkv))
    queries = qkv[:, :attn_width].reshape(SLOTS, HEADS, HEAD_DIM)
    key_vals = qkv[:, attn_width:attn_width + kv_width].reshape(SLOTS, KV_HEADS, HEAD_DIM)
    value_vals = qkv[:, attn_width + kv_width:].reshape(SLOTS, KV_HEADS, HEAD_DIM)
    queries = low(rotate(queries, cosine, sine_table))
    key_vals = low(rotate(key_vals, cosine, sine_table))
    value_vals = low(value_vals)
    query_blocks = queries.reshape(block_count, block_rows, KV_HEADS, group_size, HEAD_DIM)
    block_starts = jnp.arange(block_count, dtype=jnp.int32) * block_rows

    def attend(block_item):
        query_block, block_start = block_item
        raw_scores = low_back(jnp.einsum('qkgd,skd->kgqs', query_block, key_vals, precision=PRECISE))
        scores = raw_scores * SCORE_SCALE
        query_slots = block_start + jnp.arange(block_rows, dtype=jnp.int32)
        allowed = (positions[None, :] <= query_slots[:, None]) & (positions[None, :] < length)
        scores = jnp.where(allowed[None, None], scores, -1e+30)
        probabilities = low(jax.nn.softmax(scores, axis=-1))
        return jnp.einsum('kgqs,skd->qkgd', probabilities, value_vals, precision=PRECISE)
    attn_out = lax.map(jax.checkpoint(attend), (query_blocks, block_starts))
    attended = low(low_back(attn_out.reshape(SLOTS, attn_width)))
    branch = low_back(matmul(attended, w_out))
    hidden = seq_tokens + RESIDUAL_SCALE * branch
    normed2 = low(rms_norm(hidden, gains[:, 1]))
    gate_up = low_back(matmul(normed2, w_gate_up))
    mixed_vals = low(jax.nn.silu(gate_up[:, :FF]) * gate_up[:, FF:])
    down_out = low_back(matmul(mixed_vals, w_down))
    return valid_rows * (hidden + RESIDUAL_SCALE * down_out)

def reference(tokens, lengths, w_qkv, w_out, w_gate_up, w_down, gains, cotangent):
    weights = tuple((weight.astype(jnp.float32) for weight in (w_qkv, w_out, w_gate_up, w_down, gains)))

    def per_sequence(running, sequence_item):
        seq_tokens, length, seq_cotangent = sequence_item

        def forward(inputs, first_w, second_w, third_w, fourth_w, gain_w):
            return layer(inputs, first_w, second_w, third_w, fourth_w, gain_w, length)
        result, pullback = jax.vjp(forward, seq_tokens.astype(jnp.float32), weights[0], weights[1], weights[2], weights[3], weights[4])
        gradients = pullback(seq_cotangent.astype(jnp.float32))
        updated = tuple((total_grad + new_grad for total_grad, new_grad in zip(running, gradients[1:])))
        return (updated, (result.astype(jnp.bfloat16), gradients[0]))
    zero_grads = tuple((jnp.zeros(weight.shape, jnp.float32) for weight in weights))
    totals, (outputs, token_grads) = lax.scan(per_sequence, zero_grads, (tokens, lengths, cotangent))
    return (outputs, token_grads, totals[0], totals[1], totals[2], totals[3], totals[4])
```

```python
import functools

import jax
import jax.numpy as jnp
from jax import lax
from jax.experimental import pallas as pl
from jax.experimental.pallas import tpu as pltpu
from jax.sharding import PartitionSpec as P

HEADS = 32
KV_HEADS = 8
HEAD_DIM = 64
FF = 8192
ATTN = HEADS * HEAD_DIM
KV = KV_HEADS * HEAD_DIM
PAIR = 2 * HEAD_DIM

EPSILON = 1e-05
RESIDUAL_SCALE = 0.22
SCORE_SCALE = 1.0 / 64.0
ROPE_THETA = 10000000.0
BLOCK = 256

BF16 = jnp.bfloat16
F32 = jnp.float32


def dot(left, right):
    return jnp.dot(left, right, preferred_element_type=F32)


def dot_nt(left, right):
    return lax.dot_general(left, right, (((1,), (1,)), ((), ())), preferred_element_type=F32)


def dot_tn(left, right):
    return lax.dot_general(left, right, (((0,), (0,)), ((), ())), preferred_element_type=F32)


tie = lax.optimization_barrier


def rotary_pair(slots):
    half_dim = HEAD_DIM // 2
    frequency = ROPE_THETA ** (-(jnp.arange(half_dim, dtype=F32) * 2.0) / HEAD_DIM)
    angles = jnp.arange(slots, dtype=jnp.int32).astype(F32)[:, None] * frequency[None, :]
    angles = jnp.concatenate([angles] * 4, axis=1)
    return (jnp.cos(angles), jnp.sin(angles))


def turn(values):
    half = HEAD_DIM // 2
    lane = lax.broadcasted_iota(jnp.int32, values.shape, 1) % HEAD_DIM
    ahead = pltpu.roll(values, PAIR - half, 1)
    behind = pltpu.roll(values, half, 1)
    return jnp.where(lane < half, -ahead, behind)


def left_lanes(shape):
    return lax.broadcasted_iota(jnp.int32, shape, 1) < HEAD_DIM


def mask_bias(start, block, stop, length):
    key = lax.broadcasted_iota(jnp.int32, (stop, block), 0)
    query = lax.broadcasted_iota(jnp.int32, (stop, block), 1) + start
    return jnp.where((key <= query) & (key < length), 0.0, -1e30)


def attend_kernel(block, length_ref, qkv_ref, cos_ref, sin_ref, out_ref, q_ref, k_ref, v_ref, lse_ref):
    slots = qkv_ref.shape[0]
    pairs = q_ref.shape[1] // PAIR
    length = length_ref[0]
    cosine, sine = cos_ref[...], sin_ref[...]
    for pair in range(pairs):
        lanes = slice(pair * PAIR, (pair + 1) * PAIR)
        values = qkv_ref[:, lanes]
        rotated = (values * cosine + turn(values) * sine).astype(BF16)
        q_ref[:, lanes] = rotated * jnp.asarray(SCORE_SCALE, BF16)
    values = qkv_ref[:, pairs * PAIR :]
    left = left_lanes(values.shape)
    swapped = pltpu.roll(values, HEAD_DIM, 1)
    keys = jnp.where(left, values, swapped)
    k_ref[...] = (keys * cosine + turn(keys) * sine).astype(BF16)
    v_both = jnp.where(left, swapped, values)
    v_ref[...] = v_both.astype(BF16)
    v_t = v_both.T.astype(BF16)
    lse_ref[...] = jnp.zeros_like(lse_ref)
    for start in range(0, slots, block):
        stop = start + block
        rows = slice(start, stop)
        bias = mask_bias(start, block, stop, length)
        keys = k_ref[:stop]
        for pair in range(pairs):
            lanes = slice(pair * PAIR, (pair + 1) * PAIR)
            queries = q_ref[rows, lanes]
            left = left_lanes(queries.shape)
            outs = []
            for side in range(2):
                query = jnp.where(left == (side == 0), queries, jnp.zeros_like(queries))
                scores = dot_nt(keys, query) + bias
                largest = jnp.max(scores, axis=0, keepdims=True)
                weights = jnp.exp(scores - largest)
                total = jnp.sum(weights, axis=0, keepdims=True)
                head = 2 * pair + side
                lse_ref[head : head + 1, rows] = largest + jnp.log(total)
                probabilities = (weights * (1.0 / total)).astype(BF16)
                outs.append(dot(v_t[:, :stop], probabilities))
            first = lax.broadcasted_iota(jnp.int32, outs[0].shape, 0) < HEAD_DIM
            out_ref[rows, lanes] = jnp.where(first, outs[0], outs[1]).T.astype(BF16)


def attend(qkv, cosine, sine, lengths, q_width):
    slots = qkv.shape[0]
    block = min(BLOCK, slots)
    full = pl.BlockSpec(memory_space=pltpu.VMEM)
    shape = jax.ShapeDtypeStruct
    return pl.pallas_call(
        functools.partial(attend_kernel, block),
        out_shape=(
            shape((slots, q_width), BF16),
            shape((slots, q_width), BF16),
            shape((slots, PAIR), BF16),
            shape((slots, PAIR), BF16),
            shape((8, slots), F32),
        ),
        in_specs=[pl.BlockSpec(memory_space=pltpu.SMEM), full, full, full],
        out_specs=(full,) * 5,
        compiler_params=pltpu.CompilerParams(vmem_limit_bytes=48 << 20),
        cost_estimate=pl.CostEstimate(
            flops=4 * slots * slots * q_width, bytes_accessed=12 * slots * q_width,
            transcendentals=slots * slots * q_width // HEAD_DIM,
        ),
    )(lengths, qkv, cosine, sine)


def attend_back_kernel(
    block, length_ref, q_ref, k_ref, v_ref, lse_ref, grad_ref, cos_ref, sin_ref, out_ref, dk_ref, dv_ref
):
    slots = q_ref.shape[0]
    pairs = q_ref.shape[1] // PAIR
    length = length_ref[0]
    dk_ref[...] = jnp.zeros_like(dk_ref)
    dv_ref[...] = jnp.zeros_like(dv_ref)
    k_t = k_ref[...].astype(F32).T.astype(BF16)
    for start in range(0, slots, block):
        stop = start + block
        rows = slice(start, stop)
        bias = mask_bias(start, block, stop, length)
        keys, values = k_ref[:stop], v_ref[:stop]
        for pair in range(pairs):
            lanes = slice(pair * PAIR, (pair + 1) * PAIR)
            queries, grads = q_ref[rows, lanes], grad_ref[rows, lanes]
            left = left_lanes(queries.shape)
            parts = []
            for side in range(2):
                head = 2 * pair + side
                query = jnp.where(left == (side == 0), queries, jnp.zeros_like(queries))
                grad = jnp.where(left == (side == 0), grads, jnp.zeros_like(grads))
                scores = dot_nt(keys, query) + bias
                weights = jnp.exp(scores - lse_ref[head : head + 1, rows])
                dv_ref[:stop] += dot(weights.astype(BF16), grad)
                d_weights = dot_nt(values, grad)
                row_dot = jnp.sum(weights * d_weights, axis=0, keepdims=True)
                d_scores = (weights * (d_weights - row_dot)).astype(BF16)
                dk_ref[:stop] += dot(d_scores, query)
                parts.append(dot(k_t[:, :stop], d_scores))
            first = lax.broadcasted_iota(jnp.int32, parts[0].shape, 0) < HEAD_DIM
            d_query = jnp.where(first, parts[0], parts[1]).T * SCORE_SCALE
            d_query = d_query * cos_ref[rows] - turn(d_query) * sin_ref[rows]
            out_ref[rows, lanes] = d_query.astype(BF16)
    d_key = dk_ref[...]
    d_key = d_key + pltpu.roll(d_key, HEAD_DIM, 1)
    d_key = d_key * cos_ref[...] - turn(d_key) * sin_ref[...]
    d_value = dv_ref[...]
    d_value = d_value + pltpu.roll(d_value, HEAD_DIM, 1)
    out_ref[:, pairs * PAIR :] = jnp.where(
        left_lanes(d_key.shape), d_key, d_value
    ).astype(BF16)


def attend_back(saved, grad, cosine, sine, lengths):
    query, key, value, log_sums = saved
    slots, q_width = query.shape
    block = min(BLOCK, slots)
    full = pl.BlockSpec(memory_space=pltpu.VMEM)
    return pl.pallas_call(
        functools.partial(attend_back_kernel, block),
        out_shape=jax.ShapeDtypeStruct((slots, q_width + PAIR), BF16),
        in_specs=[pl.BlockSpec(memory_space=pltpu.SMEM)] + [full] * 7,
        out_specs=full,
        scratch_shapes=[pltpu.VMEM((slots, PAIR), F32)] * 2,
        compiler_params=pltpu.CompilerParams(vmem_limit_bytes=48 << 20),
        cost_estimate=pl.CostEstimate(
            flops=10 * slots * slots * q_width, bytes_accessed=12 * slots * q_width,
            transcendentals=slots * slots * q_width // HEAD_DIM,
        ),
    )(lengths, query, key, value, log_sums, grad, cosine, sine)


def flip(mask, size):
    return [(i, i ^ mask) for i in range(size)]


def send(value, mask):
    return lax.ppermute(value, "dp", flip(mask, lax.axis_size("dp")))


def gather_near(shard):
    if lax.axis_size("dp") != 4:
        return None
    half = shard.shape[0] // 2
    top, low = shard[:half], shard[half:]
    return (send(top, 1), send(low, 1), send(top, 2), send(low, 2))


def gather_far(near):
    if near is None:
        return None
    return (send(near[0], 2), send(near[3], 1))


def place(pieces, axis):
    me = lax.axis_index("dp")
    whole = None
    for mask, piece in enumerate(pieces):
        size = piece.shape[axis]
        if whole is None:
            shape = list(piece.shape)
            shape[axis] = 4 * size
            whole = jnp.zeros(shape, piece.dtype)
        whole = lax.dynamic_update_slice_in_dim(whole, piece, (me ^ mask) * size, axis)
    return whole


def gathered(shard, near, far, axis):
    if near is None:
        return lax.all_gather(shard, "dp", axis=axis, tiled=True)
    pieces = (shard,) + tuple(
        jnp.concatenate(pair, axis=0) for pair in (near[:2], near[2:], far)
    )
    return place(pieces, axis)


def gather_direct(shard, axis):
    if lax.axis_size("dp") != 4:
        return lax.all_gather(shard, "dp", axis=axis, tiled=True)
    return place((shard, send(shard, 1), send(shard, 2), send(shard, 3)), axis)


def dp_block(partial, mask, axis):
    place = lax.axis_index("dp") ^ mask
    if partial.ndim == 2:
        size = partial.shape[1] // 4
        return lax.dynamic_slice_in_dim(partial, place * size, size, 1)
    return lax.dynamic_index_in_dim(partial, place, axis, keepdims=False)


def scatter_first(partial, axis):
    if lax.axis_size("dp") != 4:
        return lax.psum_scatter(
            partial.astype(BF16), "dp", scatter_dimension=axis, tiled=partial.ndim == 2
        )
    half = (partial.shape[0] if axis else partial.shape[1]) // 2
    beside, across, far = (dp_block(partial, mask, axis) for mask in (1, 2, 3))
    top = jnp.stack([beside[:half], far[:half]]).astype(BF16)
    low = jnp.stack([across[half:], far[half:]]).astype(BF16)
    return (send(top, 1), send(low, 2))


def scatter_second(partial, got, axis):
    if lax.axis_size("dp") != 4:
        return got.astype(F32)
    half = (partial.shape[0] if axis else partial.shape[1]) // 2
    own, beside, across = (dp_block(partial, mask, axis) for mask in (0, 1, 2))
    top, low = (part.astype(F32) for part in got)
    third = send((across[:half].astype(F32) + top[1]).astype(BF16), 2)
    fourth = send((beside[half:].astype(F32) + low[1]).astype(BF16), 1)
    return jnp.concatenate(
        [
            own[:half].astype(F32) + top[0] + third.astype(F32),
            own[half:].astype(F32) + low[0] + fourth.astype(F32),
        ],
        axis=0,
    )


def exchange(blocks, axis_name):
    return lax.all_to_all(blocks, axis_name, split_axis=0, concat_axis=0, tiled=True)


def gather_seq(shard):
    return lax.all_gather(shard, "seq", axis=0, tiled=True)


def scatter_seq(partial):
    return lax.psum_scatter(
        partial.astype(BF16), "seq", scatter_dimension=0, tiled=True
    ).astype(F32)


def gate_up_kernel(me_ref, x_ref, *refs):
    pieces, (gate_ref, up_ref, whole_out, whole, sems, out_sem) = refs[:7], refs[7:]
    me = me_ref[0]
    seqs, _, sub, ff = pieces[0].shape
    half = seqs // 2
    places = [(0, 0, seqs)] + [(mask, part * half, half) for mask in (1, 2, 3) for part in (0, 1)]
    copies = []
    for index, (piece, (mask, first, count)) in enumerate(zip(pieces, places)):
        for part in range(2):
            copies.append(
                pltpu.make_async_copy(
                    piece.at[:, part],
                    whole.at[part, pl.ds(first, count), me ^ mask],
                    sems.at[index, part],
                )
            )
    for copy in copies:
        copy.start()
    for copy in copies:
        copy.wait()
    write = pltpu.make_async_copy(whole, whole_out, out_sem)
    write.start()
    depth = whole.shape[1] * whole.shape[2] * sub
    tile = min(512, ff)
    rows = min(256, x_ref.shape[0])

    @pl.loop(0, x_ref.shape[0] // rows)
    def _(step):
        span = pl.ds(pl.multiple_of(step * rows, rows), rows)
        for start in range(0, ff, tile):
            lanes = slice(start, start + tile)
            for part, out_ref in enumerate((gate_ref, up_ref)):
                out_ref[span, lanes] = dot(
                    x_ref[span, :], whole[part, :, :, :, lanes].reshape(depth, tile)
                )

    write.wait()


def gate_up_of(normed2, pieces):
    slots = normed2.shape[0]
    seqs, parts, sub, ff = pieces[0].shape
    whole = (parts, seqs, 4, sub, ff)
    full = pl.BlockSpec(memory_space=pltpu.VMEM)
    away = pl.BlockSpec(memory_space=pl.ANY)
    shape = jax.ShapeDtypeStruct
    me = lax.axis_index("dp").astype(jnp.int32).reshape(1)
    return pl.pallas_call(
        gate_up_kernel,
        out_shape=(shape((slots, ff), F32), shape((slots, ff), F32), shape(whole, BF16)),
        in_specs=[pl.BlockSpec(memory_space=pltpu.SMEM), full] + [away] * len(pieces),
        out_specs=(full, full, away),
        scratch_shapes=[
            pltpu.VMEM(whole, BF16),
            pltpu.SemaphoreType.DMA((len(pieces), 2)),
            pltpu.SemaphoreType.DMA,
        ],
        compiler_params=pltpu.CompilerParams(vmem_limit_bytes=56 << 20),
        cost_estimate=pl.CostEstimate(
            flops=2 * slots * normed2.shape[1] * 2 * ff,
            bytes_accessed=8 * slots * ff + 8 * ff * normed2.shape[1],
            transcendentals=0,
        ),
    )(me, normed2, *pieces)


def local(tokens, lengths, w_qkv, w_out, w_gate_up, w_down, gains, cotangent):
    tok_rows, width = tokens.shape[1:]
    seqs, ranks = lax.axis_size("seq"), lax.axis_size("dp")
    slots = tok_rows * seqs
    q_width = ATTN // seqs
    repeats = max(1, seqs // KV_HEADS)
    ff = FF // seqs
    sub = w_qkv.shape[0] // ranks

    first_slot = lax.axis_index("seq") * tok_rows
    length = lengths[0]
    valid = (jnp.arange(slots, dtype=jnp.int32) < length).astype(F32)[:, None]
    valid_rows = ((first_slot + jnp.arange(tok_rows)) < length).astype(F32)[:, None]
    cosine, sine = rotary_pair(slots)

    def split_qkv(rows):
        def heads(block):
            block = block.reshape(sub, KV_HEADS, HEAD_DIM)
            return jnp.repeat(block, repeats, axis=1)

        query = rows[:, :ATTN].reshape(sub, seqs, q_width)
        joined = jnp.concatenate(
            [query, heads(rows[:, ATTN : ATTN + KV]), heads(rows[:, ATTN + KV :])], axis=2
        )
        return joined.transpose(1, 0, 2)

    def join_qkv(blocks):
        def heads(block):
            block = block.reshape(sub, KV_HEADS, repeats, HEAD_DIM)
            if repeats > 1:
                block = block.astype(F32).sum(axis=2).astype(BF16)
            return block.reshape(sub, KV)

        blocks = blocks.transpose(1, 0, 2)
        key_part = heads(blocks[:, :, q_width : q_width + HEAD_DIM])
        value_part = heads(blocks[:, :, q_width + HEAD_DIM :])
        return jnp.concatenate([blocks[:, :, :q_width].reshape(sub, ATTN), key_part, value_part], axis=1)

    all_tokens = gather_seq(tokens[0])
    gain_rows = jnp.broadcast_to(gains.T, (seqs, 2, gains.shape[0]))
    all_gains = exchange(gain_rows, "seq").transpose(1, 0, 2).reshape(2, width).astype(F32)
    gain_first, gain_second = all_gains[0], all_gains[1]
    qkv_rows = lax.all_to_all(w_qkv, "dp", split_axis=0, concat_axis=1, tiled=True)
    qkv_mine = exchange(split_qkv(qkv_rows), "seq")
    my_qkv = gather_direct(qkv_mine[:, None], 1).reshape(width, q_width + PAIR)
    my_out = gather_direct(w_out, 1)

    per_block = w_gate_up.shape[1] // ff
    gu_rows = exchange(
        w_gate_up.reshape(ranks, sub, per_block, ff).transpose(0, 2, 1, 3), "dp"
    )
    all_tokens, gu_rows, my_qkv, all_gains = tie((all_tokens, gu_rows, my_qkv, all_gains))
    w_down, my_qkv = tie((w_down, my_qkv))
    gain_first, gain_second = all_gains[0], all_gains[1]
    gu_mine = exchange(gu_rows.reshape(2, seqs, sub, ff).transpose(1, 0, 2, 3), "seq")
    down_near = gather_near(w_down)

    x_all = all_tokens.astype(F32)
    inv_all = lax.rsqrt(jnp.mean(x_all * x_all, axis=1, keepdims=True) + EPSILON)
    normed = (x_all * inv_all * gain_first).astype(BF16)
    qkv = dot(normed, my_qkv)
    attended, *saved = attend(qkv, cosine, sine, lengths, q_width)
    attended, gu_mine, down_near, my_out = tie((attended, gu_mine, down_near, my_out))
    gu_near = gather_near(gu_mine)

    x = tokens[0].astype(F32)
    branch = scatter_seq(dot(attended, my_out))
    branch, gu_near = tie((branch, gu_near))
    gu_far, down_far = gather_far(gu_near), gather_far(down_near)
    hidden = x + RESIDUAL_SCALE * branch
    inv_second = lax.rsqrt(jnp.mean(hidden * hidden, axis=1, keepdims=True) + EPSILON)
    unit_second = hidden * inv_second
    normed2 = gather_seq((unit_second * gain_second).astype(BF16))
    normed2, gu_far = tie((normed2, gu_far))
    my_down = gathered(w_down, down_near, down_far, 1)
    late_cotangent, normed2 = tie((cotangent[0], normed2))
    all_cotangent = gather_seq(late_cotangent)

    if gu_near is None:
        my_gate_up = lax.all_gather(gu_mine, "dp", axis=1).transpose(2, 0, 1, 3, 4)
        my_gate, my_up = (my_gate_up[part].reshape(width, ff) for part in range(2))
        gate_vals, up_vals = dot(normed2, my_gate), dot(normed2, my_up)
    else:
        gate_vals, up_vals, my_gate_up = gate_up_of(normed2, (gu_mine,) + gu_near + gu_far)
        my_gate, my_up = (my_gate_up[part].reshape(width, ff) for part in range(2))
    sigmoid_gate = jax.nn.sigmoid(gate_vals)
    mixed = (gate_vals * sigmoid_gate * up_vals).astype(BF16)
    down_grad = (RESIDUAL_SCALE * (all_cotangent.astype(F32) * valid)).astype(BF16)
    mixed_grad = dot_nt(down_grad, my_down)
    gate_grad = (
        mixed_grad * up_vals * sigmoid_gate * (1.0 + gate_vals * (1.0 - sigmoid_gate))
    ).astype(BF16)
    up_grad = (mixed_grad * gate_vals * sigmoid_gate).astype(BF16)
    normed2_grad = scatter_seq(dot_nt(gate_grad, my_gate) + dot_nt(up_grad, my_up))
    w_grads = jnp.stack([dot_tn(normed2, gate_grad), dot_tn(normed2, up_grad)])
    gu_partial = w_grads.astype(BF16).reshape(2, seqs, ranks, sub, ff).transpose(1, 0, 2, 3, 4)
    gu_got = scatter_first(gu_partial, 2)
    normed2_grad, gu_got = tie((normed2_grad, gu_got))

    upstream = cotangent[0].astype(F32) * valid_rows
    unit_grad2 = normed2_grad * gain_second
    hidden_grad = upstream + inv_second * (
        unit_grad2 - unit_second * jnp.mean(unit_grad2 * unit_second, axis=1, keepdims=True)
    )
    gain_second_term = jnp.sum(normed2_grad * unit_second, axis=0)
    branch_grad = gather_seq((RESIDUAL_SCALE * hidden_grad).astype(BF16))
    gu_summed = scatter_second(gu_partial, gu_got, 2)
    branch_grad, gu_summed, mixed = tie((branch_grad, gu_summed.astype(BF16), mixed))
    down_out = scatter_seq(dot(mixed, my_down))
    output = (valid_rows * (hidden + RESIDUAL_SCALE * down_out)).astype(BF16)

    attended_grad = dot_nt(branch_grad, my_out).astype(BF16)
    qkv_grad = attend_back(saved, attended_grad, cosine, sine, lengths)
    gu_blocks = exchange(gu_summed, "seq")
    down_partial = dot_tn(mixed, down_grad).astype(BF16)
    down_got = scatter_first(down_partial, 1)
    qkv_grad, down_got = tie((qkv_grad, down_got))
    normed_partial = dot_nt(qkv_grad, my_qkv)
    normed_grad = scatter_seq(normed_partial)

    qkv_partial = dot_tn(normed, qkv_grad).astype(BF16).reshape(seqs, ranks, sub, -1)
    qkv_summed = scatter_second(qkv_partial, scatter_first(qkv_partial, 1), 1)
    qkv_back = join_qkv(exchange(qkv_summed.astype(BF16), "seq"))
    grad_qkv = lax.all_to_all(qkv_back, "dp", split_axis=1, concat_axis=0, tiled=True).astype(F32)
    out_partial = dot_tn(attended, branch_grad).astype(BF16)
    grad_out = scatter_second(out_partial, scatter_first(out_partial, 1), 1)
    grad_down = scatter_second(down_partial, down_got, 1)
    gu_back = exchange(
        gu_blocks.transpose(1, 0, 2, 3).reshape(ranks, per_block, sub, ff), "dp"
    )
    grad_gate_up = gu_back.transpose(0, 2, 1, 3).reshape(w_gate_up.shape).astype(F32)

    unit_all = x_all * inv_all
    gain_first_term = jnp.sum(normed_partial * unit_all, axis=0)
    gains_term = jnp.stack([gain_first_term, gain_second_term], axis=1)
    gain_blocks = exchange(gains_term.reshape(seqs, -1, 2), "seq")
    grad_gains = jnp.sum(gain_blocks, axis=0).T
    if ranks == 4:
        grad_gains = grad_gains + send(grad_gains, 1)
        grad_gains = (grad_gains + send(grad_gains, 2)).T
    else:
        grad_gains = lax.psum(grad_gains, "dp").T

    inv_first = lax.rsqrt(jnp.mean(x * x, axis=1, keepdims=True) + EPSILON)
    unit_first = x * inv_first
    unit_grad1 = normed_grad * gain_first
    token_grad = hidden_grad + inv_first * (
        unit_grad1 - unit_first * jnp.mean(unit_grad1 * unit_first, axis=1, keepdims=True)
    )
    return (output[None], token_grad[None], grad_qkv, grad_out, grad_gate_up, grad_down, grad_gains)


def solution(mesh):
    in_specs = (
        P("dp", "seq", None),
        P("dp"),
        P("seq", "dp"),
        P("seq", "dp"),
        P("seq", "dp"),
        P("seq", "dp"),
        P("seq", None),
        P("dp", "seq", None),
    )
    out_specs = (
        P("dp", "seq", None),
        P("dp", "seq", None),
        P("seq", "dp"),
        P("seq", "dp"),
        P("seq", "dp"),
        P("seq", "dp"),
        P("seq", None),
    )
    return jax.shard_map(local, mesh=mesh, in_specs=in_specs, out_specs=out_specs, check_vma=False)
```

```python
import functools

import jax
import jax.numpy as jnp
from jax import lax
from jax.experimental import pallas as pl
from jax.experimental.pallas import tpu as pltpu
from jax.sharding import PartitionSpec as P

HEADS = 32
KV_HEADS = 8
HEAD_DIM = 64
FF = 8192
ATTN = HEADS * HEAD_DIM
KV = KV_HEADS * HEAD_DIM
PAIR = 2 * HEAD_DIM

EPSILON = 1e-05
RESIDUAL_SCALE = 0.22
SCORE_SCALE = 1.0 / 64.0
ROPE_THETA = 10000000.0
BLOCK = 256

BF16 = jnp.bfloat16
F32 = jnp.float32


def dot(left, right):
    return jnp.dot(left, right, preferred_element_type=F32)


def dot_nt(left, right):
    return lax.dot_general(left, right, (((1,), (1,)), ((), ())), preferred_element_type=F32)


def dot_tn(left, right):
    return lax.dot_general(left, right, (((0,), (0,)), ((), ())), preferred_element_type=F32)


tie = lax.optimization_barrier


def rotary_pair(slots):
    half_dim = HEAD_DIM // 2
    frequency = ROPE_THETA ** (-(jnp.arange(half_dim, dtype=F32) * 2.0) / HEAD_DIM)
    angles = jnp.arange(slots, dtype=jnp.int32).astype(F32)[:, None] * frequency[None, :]
    angles = jnp.concatenate([angles] * 4, axis=1)
    return (jnp.cos(angles), jnp.sin(angles))


def turn(values):
    half = HEAD_DIM // 2
    lane = lax.broadcasted_iota(jnp.int32, values.shape, 1) % HEAD_DIM
    ahead = pltpu.roll(values, PAIR - half, 1)
    behind = pltpu.roll(values, half, 1)
    return jnp.where(lane < half, -ahead, behind)


def left_lanes(shape):
    return lax.broadcasted_iota(jnp.int32, shape, 1) < HEAD_DIM


def mask_bias(start, block, stop, length):
    key = lax.broadcasted_iota(jnp.int32, (stop, block), 0)
    query = lax.broadcasted_iota(jnp.int32, (stop, block), 1) + start
    return jnp.where((key <= query) & (key < length), 0.0, -1e30)


def attend_kernel(block, length_ref, qkv_ref, cos_ref, sin_ref, out_ref, q_ref, k_ref, v_ref, lse_ref):
    slots = qkv_ref.shape[0]
    pairs = q_ref.shape[1] // PAIR
    length = length_ref[0]
    cosine, sine = cos_ref[...], sin_ref[...]
    for pair in range(pairs):
        lanes = slice(pair * PAIR, (pair + 1) * PAIR)
        values = qkv_ref[:, lanes]
        rotated = (values * cosine + turn(values) * sine).astype(BF16)
        q_ref[:, lanes] = rotated * jnp.asarray(SCORE_SCALE, BF16)
    values = qkv_ref[:, pairs * PAIR :]
    left = left_lanes(values.shape)
    swapped = pltpu.roll(values, HEAD_DIM, 1)
    keys = jnp.where(left, values, swapped)
    k_ref[...] = (keys * cosine + turn(keys) * sine).astype(BF16)
    v_both = jnp.where(left, swapped, values)
    v_ref[...] = v_both.astype(BF16)
    v_t = v_both.T.astype(BF16)
    lse_ref[...] = jnp.zeros_like(lse_ref)
    for start in range(0, slots, block):
        stop = start + block
        rows = slice(start, stop)
        bias = mask_bias(start, block, stop, length)
        keys = k_ref[:stop]
        for pair in range(pairs):
            lanes = slice(pair * PAIR, (pair + 1) * PAIR)
            queries = q_ref[rows, lanes]
            left = left_lanes(queries.shape)
            outs = []
            for side in range(2):
                query = jnp.where(left == (side == 0), queries, jnp.zeros_like(queries))
                scores = dot_nt(keys, query) + bias
                largest = jnp.max(scores, axis=0, keepdims=True)
                weights = jnp.exp(scores - largest)
                total = jnp.sum(weights, axis=0, keepdims=True)
                head = 2 * pair + side
                lse_ref[head : head + 1, rows] = largest + jnp.log(total)
                probabilities = (weights * (1.0 / total)).astype(BF16)
                outs.append(dot(v_t[:, :stop], probabilities))
            first = lax.broadcasted_iota(jnp.int32, outs[0].shape, 0) < HEAD_DIM
            out_ref[rows, lanes] = jnp.where(first, outs[0], outs[1]).T.astype(BF16)


def attend(qkv, cosine, sine, lengths, q_width):
    slots = qkv.shape[0]
    block = min(BLOCK, slots)
    full = pl.BlockSpec(memory_space=pltpu.VMEM)
    shape = jax.ShapeDtypeStruct
    return pl.pallas_call(
        functools.partial(attend_kernel, block),
        out_shape=(
            shape((slots, q_width), BF16),
            shape((slots, q_width), BF16),
            shape((slots, PAIR), BF16),
            shape((slots, PAIR), BF16),
            shape((8, slots), F32),
        ),
        in_specs=[pl.BlockSpec(memory_space=pltpu.SMEM), full, full, full],
        out_specs=(full,) * 5,
        compiler_params=pltpu.CompilerParams(vmem_limit_bytes=48 << 20),
        cost_estimate=pl.CostEstimate(
            flops=4 * slots * slots * q_width, bytes_accessed=12 * slots * q_width,
            transcendentals=slots * slots * q_width // HEAD_DIM,
        ),
    )(lengths, qkv, cosine, sine)


def attend_back_kernel(
    block, length_ref, q_ref, k_ref, v_ref, lse_ref, grad_ref, cos_ref, sin_ref, out_ref, dk_ref, dv_ref
):
    slots = q_ref.shape[0]
    pairs = q_ref.shape[1] // PAIR
    length = length_ref[0]
    dk_ref[...] = jnp.zeros_like(dk_ref)
    dv_ref[...] = jnp.zeros_like(dv_ref)
    k_t = k_ref[...].astype(F32).T.astype(BF16)
    for start in range(0, slots, block):
        stop = start + block
        rows = slice(start, stop)
        bias = mask_bias(start, block, stop, length)
        keys, values = k_ref[:stop], v_ref[:stop]
        for pair in range(pairs):
            lanes = slice(pair * PAIR, (pair + 1) * PAIR)
            queries, grads = q_ref[rows, lanes], grad_ref[rows, lanes]
            left = left_lanes(queries.shape)
            parts = []
            for side in range(2):
                head = 2 * pair + side
                query = jnp.where(left == (side == 0), queries, jnp.zeros_like(queries))
                grad = jnp.where(left == (side == 0), grads, jnp.zeros_like(grads))
                scores = dot_nt(keys, query) + bias
                weights = jnp.exp(scores - lse_ref[head : head + 1, rows])
                dv_ref[:stop] += dot(weights.astype(BF16), grad)
                d_weights = dot_nt(values, grad)
                row_dot = jnp.sum(weights * d_weights, axis=0, keepdims=True)
                d_scores = (weights * (d_weights - row_dot)).astype(BF16)
                dk_ref[:stop] += dot(d_scores, query)
                parts.append(dot(k_t[:, :stop], d_scores))
            first = lax.broadcasted_iota(jnp.int32, parts[0].shape, 0) < HEAD_DIM
            d_query = jnp.where(first, parts[0], parts[1]).T * SCORE_SCALE
            d_query = d_query * cos_ref[rows] - turn(d_query) * sin_ref[rows]
            out_ref[rows, lanes] = d_query.astype(BF16)
    d_key = dk_ref[...]
    d_key = d_key + pltpu.roll(d_key, HEAD_DIM, 1)
    d_key = d_key * cos_ref[...] - turn(d_key) * sin_ref[...]
    d_value = dv_ref[...]
    d_value = d_value + pltpu.roll(d_value, HEAD_DIM, 1)
    out_ref[:, pairs * PAIR :] = jnp.where(
        left_lanes(d_key.shape), d_key, d_value
    ).astype(BF16)


def attend_back(saved, grad, cosine, sine, lengths):
    query, key, value, log_sums = saved
    slots, q_width = query.shape
    block = min(BLOCK, slots)
    full = pl.BlockSpec(memory_space=pltpu.VMEM)
    return pl.pallas_call(
        functools.partial(attend_back_kernel, block),
        out_shape=jax.ShapeDtypeStruct((slots, q_width + PAIR), BF16),
        in_specs=[pl.BlockSpec(memory_space=pltpu.SMEM)] + [full] * 7,
        out_specs=full,
        scratch_shapes=[pltpu.VMEM((slots, PAIR), F32)] * 2,
        compiler_params=pltpu.CompilerParams(vmem_limit_bytes=48 << 20),
        cost_estimate=pl.CostEstimate(
            flops=10 * slots * slots * q_width, bytes_accessed=12 * slots * q_width,
            transcendentals=slots * slots * q_width // HEAD_DIM,
        ),
    )(lengths, query, key, value, log_sums, grad, cosine, sine)


def flip(mask, size):
    return [(i, i ^ mask) for i in range(size)]


def send(value, mask):
    return lax.ppermute(value, "dp", flip(mask, lax.axis_size("dp")))


def other(first):
    return 3 - first


def gather_near(shard, first):
    if lax.axis_size("dp") != 4:
        return None
    return (send(shard, first), send(shard, other(first)))


def gather_far(near, first):
    return None if near is None else send(near[0], other(first))


def place(pieces, masks, axis):
    me = lax.axis_index("dp")
    whole = None
    for mask, piece in zip(masks, pieces):
        size = piece.shape[axis]
        if whole is None:
            shape = list(piece.shape)
            shape[axis] = 4 * size
            whole = jnp.zeros(shape, piece.dtype)
        whole = lax.dynamic_update_slice_in_dim(whole, piece, (me ^ mask) * size, axis)
    return whole


def gather_direct(shard, axis):
    if lax.axis_size("dp") != 4:
        return lax.all_gather(shard, "dp", axis=axis, tiled=True)
    return place((shard, send(shard, 1), send(shard, 2), send(shard, 3)), range(4), axis)


def dp_block(partial, mask, axis):
    place = lax.axis_index("dp") ^ mask
    if partial.ndim == 2:
        size = partial.shape[1] // 4
        return lax.dynamic_slice_in_dim(partial, place * size, size, 1)
    return lax.dynamic_index_in_dim(partial, place, axis, keepdims=False)


def gather_halves(shard, near):
    if lax.axis_size("dp") != 4:
        return None
    half = shard.shape[0] // 2
    if near is None:
        return tuple(send(part, mask) for mask in (1, 2) for part in (shard[:half], shard[half:]))
    return (send(near[0], 2), send(near[3], 1))


def join_halves(shard, near, far, axis):
    if near is None:
        return lax.all_gather(shard, "dp", axis=axis, tiled=True)
    pieces = (shard,) + tuple(
        jnp.concatenate(pair, axis=0) for pair in (near[:2], near[2:], far)
    )
    return place(pieces, range(4), axis)


def scatter_first(partial, axis, first):
    if lax.axis_size("dp") != 4:
        return lax.psum_scatter(
            partial.astype(BF16), "dp", scatter_dimension=axis, tiled=partial.ndim == 2
        )
    return send(dp_block(partial, 3, axis).astype(BF16), first)


def scatter_second(partial, got, axis, first):
    if lax.axis_size("dp") != 4:
        return got.astype(F32)
    beside = send(dp_block(partial, first, axis).astype(BF16), first)
    passed = dp_block(partial, other(first), axis).astype(F32) + got.astype(F32)
    last = send(passed.astype(BF16), other(first))
    own = dp_block(partial, 0, axis).astype(F32)
    return own + beside.astype(F32) + last.astype(F32)


def scatter_direct(partial, axis):
    if lax.axis_size("dp") != 4:
        return scatter_second(partial, scatter_first(partial, axis, 1), axis, 1)
    own = dp_block(partial, 0, axis).astype(F32)
    parts = [send(dp_block(partial, mask, axis).astype(BF16), mask) for mask in (1, 2, 3)]
    return own + parts[0].astype(F32) + parts[1].astype(F32) + parts[2].astype(F32)


def swap_dp(blocks):
    if lax.axis_size("dp") != 4:
        return exchange(blocks, "dp")
    parts = [dp_block(blocks, 0, 0)] + [send(dp_block(blocks, mask, 0), mask) for mask in (1, 2, 3)]
    return place([part[None] for part in parts], range(4), 0)


def exchange(blocks, axis_name):
    return lax.all_to_all(blocks, axis_name, split_axis=0, concat_axis=0, tiled=True)


def gather_seq(shard):
    return lax.all_gather(shard, "seq", axis=0, tiled=True)


def scatter_seq(partial):
    return lax.psum_scatter(
        partial.astype(BF16), "seq", scatter_dimension=0, tiled=True
    ).astype(F32)


def gate_up_kernel(me_ref, x_ref, *refs):
    pieces, (gate_ref, up_ref, whole_out, whole, sems, out_sem) = refs[:8], refs[8:]
    me = me_ref[0]
    sub, ff = pieces[0].shape[1:]
    copies = []
    for index, piece in enumerate(pieces):
        part, mask = divmod(index, 4)
        copies.append(
            pltpu.make_async_copy(piece, whole.at[part, :, me ^ mask], sems.at[index])
        )
    for copy in copies:
        copy.start()
    for copy in copies:
        copy.wait()
    write = pltpu.make_async_copy(whole, whole_out, out_sem)
    write.start()
    depth = whole.shape[1] * whole.shape[2] * sub
    tile = min(512, ff)
    rows = min(256, x_ref.shape[0])

    @pl.loop(0, x_ref.shape[0] // rows)
    def _(step):
        span = pl.ds(pl.multiple_of(step * rows, rows), rows)
        for start in range(0, ff, tile):
            lanes = slice(start, start + tile)
            for part, out_ref in enumerate((gate_ref, up_ref)):
                out_ref[span, lanes] = dot(
                    x_ref[span, :], whole[part, :, :, :, lanes].reshape(depth, tile)
                )

    write.wait()


def gate_up_of(normed2, pieces):
    slots = normed2.shape[0]
    seqs, sub, ff = pieces[0].shape
    whole = (2, seqs, 4, sub, ff)
    full = pl.BlockSpec(memory_space=pltpu.VMEM)
    away = pl.BlockSpec(memory_space=pl.ANY)
    shape = jax.ShapeDtypeStruct
    me = lax.axis_index("dp").astype(jnp.int32).reshape(1)
    return pl.pallas_call(
        gate_up_kernel,
        out_shape=(shape((slots, ff), F32), shape((slots, ff), F32), shape(whole, BF16)),
        in_specs=[pl.BlockSpec(memory_space=pltpu.SMEM), full] + [away] * len(pieces),
        out_specs=(full, full, away),
        scratch_shapes=[
            pltpu.VMEM(whole, BF16),
            pltpu.SemaphoreType.DMA((len(pieces),)),
            pltpu.SemaphoreType.DMA,
        ],
        compiler_params=pltpu.CompilerParams(vmem_limit_bytes=56 << 20),
        cost_estimate=pl.CostEstimate(
            flops=2 * slots * normed2.shape[1] * 2 * ff,
            bytes_accessed=8 * slots * ff + 8 * ff * normed2.shape[1],
            transcendentals=0,
        ),
    )(me, normed2, *pieces)


def local(tokens, lengths, w_qkv, w_out, w_gate_up, w_down, gains, cotangent):
    tok_rows, width = tokens.shape[1:]
    seqs, ranks = lax.axis_size("seq"), lax.axis_size("dp")
    slots = tok_rows * seqs
    q_width = ATTN // seqs
    repeats = max(1, seqs // KV_HEADS)
    ff = FF // seqs
    sub = w_qkv.shape[0] // ranks

    first_slot = lax.axis_index("seq") * tok_rows
    length = lengths[0]
    valid = (jnp.arange(slots, dtype=jnp.int32) < length).astype(F32)[:, None]
    valid_rows = ((first_slot + jnp.arange(tok_rows)) < length).astype(F32)[:, None]
    cosine, sine = rotary_pair(slots)

    def split_qkv(rows):
        def heads(block):
            block = block.reshape(sub, KV_HEADS, HEAD_DIM)
            return jnp.repeat(block, repeats, axis=1)

        query = rows[:, :ATTN].reshape(sub, seqs, q_width)
        joined = jnp.concatenate(
            [query, heads(rows[:, ATTN : ATTN + KV]), heads(rows[:, ATTN + KV :])], axis=2
        )
        return joined.transpose(1, 0, 2)

    def join_qkv(blocks):
        def heads(block):
            block = block.reshape(sub, KV_HEADS, repeats, HEAD_DIM)
            if repeats > 1:
                block = block.astype(F32).sum(axis=2).astype(BF16)
            return block.reshape(sub, KV)

        blocks = blocks.transpose(1, 0, 2)
        key_part = heads(blocks[:, :, q_width : q_width + HEAD_DIM])
        value_part = heads(blocks[:, :, q_width + HEAD_DIM :])
        return jnp.concatenate([blocks[:, :, :q_width].reshape(sub, ATTN), key_part, value_part], axis=1)

    all_tokens = gather_seq(tokens[0])
    qkv_rows = swap_dp(w_qkv.reshape(ranks, sub, -1)).transpose(1, 0, 2).reshape(sub, -1)
    per_block = w_gate_up.shape[1] // ff
    gu_rows = swap_dp(
        w_gate_up.reshape(ranks, sub, per_block, ff).transpose(0, 2, 1, 3)
    ).reshape(2, seqs, sub, ff)
    qkv_mine = exchange(split_qkv(qkv_rows), "seq")
    qkv_mine, gu_rows = tie((qkv_mine, gu_rows))
    gu_mine = exchange(gu_rows.transpose(1, 0, 2, 3), "seq")
    all_tokens, late_gains = tie((all_tokens, gains.T.reshape(1, -1)))
    all_gains = gather_seq(late_gains).reshape(seqs, 2, -1).transpose(1, 0, 2)
    all_gains = all_gains.reshape(2, width).astype(F32)
    gain_first, gain_second = all_gains[0], all_gains[1]
    my_qkv = gather_direct(qkv_mine[:, None], 1).reshape(width, q_width + PAIR)
    my_qkv, w_out, w_down = tie((my_qkv, w_out, w_down))
    my_out = gather_direct(w_out, 1)
    down_near = gather_halves(w_down, None)

    x_all = all_tokens.astype(F32)
    inv_all = lax.rsqrt(jnp.mean(x_all * x_all, axis=1, keepdims=True) + EPSILON)
    normed = (x_all * inv_all * gain_first).astype(BF16)
    qkv = dot(normed, my_qkv)
    attended, *saved = attend(qkv, cosine, sine, lengths, q_width)
    attended, gu_mine, my_out, down_near = tie((attended, gu_mine, my_out, down_near))
    gate_mine, up_mine = gu_mine[:, 0], gu_mine[:, 1]
    gate_near, up_near = gather_near(gate_mine, 1), gather_near(up_mine, 2)

    x = tokens[0].astype(F32)
    branch = scatter_seq(dot(attended, my_out))
    branch, gate_near, up_near, down_near = tie((branch, gate_near, up_near, down_near))
    gate_far, up_far = gather_far(gate_near, 1), gather_far(up_near, 2)
    down_far = gather_halves(w_down, down_near)
    hidden = x + RESIDUAL_SCALE * branch
    inv_second = lax.rsqrt(jnp.mean(hidden * hidden, axis=1, keepdims=True) + EPSILON)
    unit_second = hidden * inv_second
    normed2 = gather_seq((unit_second * gain_second).astype(BF16))
    normed2, gate_far, up_far, down_far, late_cotangent = tie(
        (normed2, gate_far, up_far, down_far, cotangent[0])
    )
    all_cotangent = gather_seq(late_cotangent)
    my_down = join_halves(w_down, down_near, down_far, 1)

    if gate_near is None:
        my_gate, my_up = (
            lax.all_gather(mine, "dp", axis=1).reshape(width, ff) for mine in (gate_mine, up_mine)
        )
        gate_vals, up_vals = dot(normed2, my_gate), dot(normed2, my_up)
    else:
        pieces = (gate_mine, *gate_near, gate_far, up_mine, up_near[1], up_near[0], up_far)
        gate_vals, up_vals, my_gate_up = gate_up_of(normed2, pieces)
        my_gate, my_up = (my_gate_up[part].reshape(width, ff) for part in range(2))
    sigmoid_gate = jax.nn.sigmoid(gate_vals)
    mixed = (gate_vals * sigmoid_gate * up_vals).astype(BF16)
    down_sum = dot(mixed, my_down).astype(BF16)
    all_cotangent, down_sum = tie((all_cotangent, down_sum))
    down_out = scatter_seq(down_sum)
    down_grad = (RESIDUAL_SCALE * (all_cotangent.astype(F32) * valid)).astype(BF16)
    mixed_grad = dot_nt(down_grad, my_down)
    gate_grad = (
        mixed_grad * up_vals * sigmoid_gate * (1.0 + gate_vals * (1.0 - sigmoid_gate))
    ).astype(BF16)
    up_grad = (mixed_grad * gate_vals * sigmoid_gate).astype(BF16)
    normed2_sum = (dot_nt(gate_grad, my_gate) + dot_nt(up_grad, my_up)).astype(BF16)
    normed2_sum, down_out = tie((normed2_sum, down_out))
    normed2_grad = scatter_seq(normed2_sum)

    gate_partial = dot_tn(normed2, gate_grad).astype(BF16).reshape(seqs, ranks, sub, ff)
    gate_got = scatter_first(gate_partial, 1, 1)
    up_partial = dot_tn(normed2, up_grad).astype(BF16).reshape(seqs, ranks, sub, ff)
    up_got = scatter_first(up_partial, 1, 2)
    down_partial = dot_tn(mixed, down_grad).astype(BF16)
    normed2_grad, gate_partial, up_partial, gate_got, up_got, down_partial = tie(
        (normed2_grad, gate_partial, up_partial, gate_got, up_got, down_partial)
    )

    upstream = cotangent[0].astype(F32) * valid_rows
    unit_grad2 = normed2_grad * gain_second
    hidden_grad = upstream + inv_second * (
        unit_grad2 - unit_second * jnp.mean(unit_grad2 * unit_second, axis=1, keepdims=True)
    )
    gain_second_term = jnp.sum(normed2_grad * unit_second, axis=0)
    branch_grad = gather_seq((RESIDUAL_SCALE * hidden_grad).astype(BF16))
    gate_summed = scatter_second(gate_partial, gate_got, 1, 1).astype(BF16)
    up_summed = scatter_second(up_partial, up_got, 1, 2).astype(BF16)
    branch_grad, gate_summed, up_summed, down_partial = tie(
        (branch_grad, gate_summed, up_summed, down_partial)
    )
    gu_blocks = exchange(jnp.stack([gate_summed, up_summed], axis=1), "seq")
    grad_down = scatter_direct(down_partial, 1)

    attended_grad = dot_nt(branch_grad, my_out).astype(BF16)
    qkv_grad = attend_back(saved, attended_grad, cosine, sine, lengths)
    normed_partial = dot_nt(qkv_grad, my_qkv)
    normed_sum, gu_blocks, grad_down = tie((normed_partial.astype(BF16), gu_blocks, grad_down))
    normed_grad = scatter_seq(normed_sum)

    qkv_grad, attended, normed_partial = tie((qkv_grad, attended, normed_partial))
    qkv_partial = dot_tn(normed, qkv_grad).astype(BF16).reshape(seqs, ranks, sub, -1)
    qkv_summed = scatter_direct(qkv_partial, 1).astype(BF16)
    out_partial = dot_tn(attended, branch_grad).astype(BF16)
    grad_out = scatter_direct(out_partial, 1)
    qkv_back = join_qkv(exchange(qkv_summed, "seq"))
    grad_qkv = (
        swap_dp(qkv_back.reshape(sub, ranks, -1).transpose(1, 0, 2))
        .reshape(w_qkv.shape)
        .astype(F32)
    )
    gu_back = swap_dp(
        gu_blocks.transpose(1, 0, 2, 3).reshape(ranks, per_block, sub, ff)
    )
    grad_gate_up = gu_back.transpose(0, 2, 1, 3).reshape(w_gate_up.shape).astype(F32)

    unit_all = x_all * inv_all
    gain_first_term = jnp.sum(normed_partial * unit_all, axis=0)
    gains_term = jnp.stack([gain_first_term, gain_second_term]).reshape(2, seqs, -1)
    gain_blocks = exchange(gains_term.transpose(1, 0, 2), "seq")
    grad_gains = jnp.sum(gain_blocks, axis=0)
    if ranks == 4:
        grad_gains = grad_gains + send(grad_gains, 1)
        grad_gains = (grad_gains + send(grad_gains, 2)).T
    else:
        grad_gains = lax.psum(grad_gains, "dp").T

    normed_grad, grad_qkv, grad_out, grad_gate_up, grad_gains = tie(
        (normed_grad, grad_qkv, grad_out, grad_gate_up, grad_gains)
    )
    output = (valid_rows * (hidden + RESIDUAL_SCALE * down_out)).astype(BF16)
    inv_first = lax.rsqrt(jnp.mean(x * x, axis=1, keepdims=True) + EPSILON)
    unit_first = x * inv_first
    unit_grad1 = normed_grad * gain_first
    token_grad = hidden_grad + inv_first * (
        unit_grad1 - unit_first * jnp.mean(unit_grad1 * unit_first, axis=1, keepdims=True)
    )
    return (output[None], token_grad[None], grad_qkv, grad_out, grad_gate_up, grad_down, grad_gains)


def solution(mesh):
    in_specs = (
        P("dp", "seq", None),
        P("dp"),
        P("seq", "dp"),
        P("seq", "dp"),
        P("seq", "dp"),
        P("seq", "dp"),
        P("seq", None),
        P("dp", "seq", None),
    )
    out_specs = (
        P("dp", "seq", None),
        P("dp", "seq", None),
        P("seq", "dp"),
        P("seq", "dp"),
        P("seq", "dp"),
        P("seq", "dp"),
        P("seq", None),
    )
    return jax.shard_map(local, mesh=mesh, in_specs=in_specs, out_specs=out_specs, check_vma=False)
```

```python
import functools

import jax
import jax.numpy as jnp
from jax import lax
from jax.experimental import pallas as pl
from jax.experimental.pallas import tpu as pltpu
from jax.sharding import PartitionSpec as P

HEADS = 32
KV_HEADS = 8
HEAD_DIM = 64
FF = 8192
ATTN = HEADS * HEAD_DIM
KV = KV_HEADS * HEAD_DIM
PAIR = 2 * HEAD_DIM

EPSILON = 1e-05
RESIDUAL_SCALE = 0.22
SCORE_SCALE = 1.0 / 64.0
ROPE_THETA = 10000000.0
BLOCK = 256

BF16 = jnp.bfloat16
F32 = jnp.float32


def dot(left, right):
    return jnp.dot(left, right, preferred_element_type=F32)


def dot_nt(left, right):
    return lax.dot_general(left, right, (((1,), (1,)), ((), ())), preferred_element_type=F32)


def dot_tn(left, right):
    return lax.dot_general(left, right, (((0,), (0,)), ((), ())), preferred_element_type=F32)


tie = lax.optimization_barrier


def rotary_pair(slots):
    half_dim = HEAD_DIM // 2
    frequency = ROPE_THETA ** (-(jnp.arange(half_dim, dtype=F32) * 2.0) / HEAD_DIM)
    angles = jnp.arange(slots, dtype=jnp.int32).astype(F32)[:, None] * frequency[None, :]
    angles = jnp.concatenate([angles] * 4, axis=1)
    return (jnp.cos(angles), jnp.sin(angles))


def turn(values):
    half = HEAD_DIM // 2
    lane = lax.broadcasted_iota(jnp.int32, values.shape, 1) % HEAD_DIM
    ahead = pltpu.roll(values, PAIR - half, 1)
    behind = pltpu.roll(values, half, 1)
    return jnp.where(lane < half, -ahead, behind)


def left_lanes(shape):
    return lax.broadcasted_iota(jnp.int32, shape, 1) < HEAD_DIM


def mask_bias(start, block, stop, length):
    key = lax.broadcasted_iota(jnp.int32, (stop, block), 0)
    query = lax.broadcasted_iota(jnp.int32, (stop, block), 1) + start
    return jnp.where((key <= query) & (key < length), 0.0, -1e30)


def attend_kernel(block, length_ref, qkv_ref, cos_ref, sin_ref, out_ref, q_ref, k_ref, v_ref, lse_ref):
    slots = qkv_ref.shape[0]
    pairs = q_ref.shape[1] // PAIR
    length = length_ref[0]
    cosine, sine = cos_ref[...], sin_ref[...]
    for pair in range(pairs):
        lanes = slice(pair * PAIR, (pair + 1) * PAIR)
        values = qkv_ref[:, lanes]
        rotated = (values * cosine + turn(values) * sine).astype(BF16)
        q_ref[:, lanes] = rotated * jnp.asarray(SCORE_SCALE, BF16)
    values = qkv_ref[:, pairs * PAIR :]
    left = left_lanes(values.shape)
    swapped = pltpu.roll(values, HEAD_DIM, 1)
    keys = jnp.where(left, values, swapped)
    k_ref[...] = (keys * cosine + turn(keys) * sine).astype(BF16)
    v_both = jnp.where(left, swapped, values)
    v_ref[...] = v_both.astype(BF16)
    v_t = v_both.T.astype(BF16)
    lse_ref[...] = jnp.zeros_like(lse_ref)
    for start in range(0, slots, block):
        stop = start + block
        rows = slice(start, stop)
        bias = mask_bias(start, block, stop, length)
        keys = k_ref[:stop]
        for pair in range(pairs):
            lanes = slice(pair * PAIR, (pair + 1) * PAIR)
            queries = q_ref[rows, lanes]
            left = left_lanes(queries.shape)
            outs = []
            for side in range(2):
                query = jnp.where(left == (side == 0), queries, jnp.zeros_like(queries))
                scores = dot_nt(keys, query) + bias
                largest = jnp.max(scores, axis=0, keepdims=True)
                weights = jnp.exp(scores - largest)
                total = jnp.sum(weights, axis=0, keepdims=True)
                head = 2 * pair + side
                lse_ref[head : head + 1, rows] = largest + jnp.log(total)
                probabilities = (weights * (1.0 / total)).astype(BF16)
                outs.append(dot(v_t[:, :stop], probabilities))
            first = lax.broadcasted_iota(jnp.int32, outs[0].shape, 0) < HEAD_DIM
            out_ref[rows, lanes] = jnp.where(first, outs[0], outs[1]).T.astype(BF16)


def attend(qkv, cosine, sine, lengths, q_width):
    slots = qkv.shape[0]
    block = min(BLOCK, slots)
    full = pl.BlockSpec(memory_space=pltpu.VMEM)
    shape = jax.ShapeDtypeStruct
    return pl.pallas_call(
        functools.partial(attend_kernel, block),
        out_shape=(
            shape((slots, q_width), BF16),
            shape((slots, q_width), BF16),
            shape((slots, PAIR), BF16),
            shape((slots, PAIR), BF16),
            shape((8, slots), F32),
        ),
        in_specs=[pl.BlockSpec(memory_space=pltpu.SMEM), full, full, full],
        out_specs=(full,) * 5,
        compiler_params=pltpu.CompilerParams(vmem_limit_bytes=48 << 20),
        cost_estimate=pl.CostEstimate(
            flops=4 * slots * slots * q_width, bytes_accessed=12 * slots * q_width,
            transcendentals=slots * slots * q_width // HEAD_DIM,
        ),
    )(lengths, qkv, cosine, sine)


def attend_back_kernel(
    block, length_ref, q_ref, k_ref, v_ref, lse_ref, grad_ref, cos_ref, sin_ref, out_ref, dk_ref, dv_ref
):
    slots = q_ref.shape[0]
    pairs = q_ref.shape[1] // PAIR
    length = length_ref[0]
    dk_ref[...] = jnp.zeros_like(dk_ref)
    dv_ref[...] = jnp.zeros_like(dv_ref)
    k_t = k_ref[...].astype(F32).T.astype(BF16)
    for start in range(0, slots, block):
        stop = start + block
        rows = slice(start, stop)
        bias = mask_bias(start, block, stop, length)
        keys, values = k_ref[:stop], v_ref[:stop]
        for pair in range(pairs):
            lanes = slice(pair * PAIR, (pair + 1) * PAIR)
            queries, grads = q_ref[rows, lanes], grad_ref[rows, lanes]
            left = left_lanes(queries.shape)
            parts = []
            for side in range(2):
                head = 2 * pair + side
                query = jnp.where(left == (side == 0), queries, jnp.zeros_like(queries))
                grad = jnp.where(left == (side == 0), grads, jnp.zeros_like(grads))
                scores = dot_nt(keys, query) + bias
                weights = jnp.exp(scores - lse_ref[head : head + 1, rows])
                dv_ref[:stop] += dot(weights.astype(BF16), grad)
                d_weights = dot_nt(values, grad)
                row_dot = jnp.sum(weights * d_weights, axis=0, keepdims=True)
                d_scores = (weights * (d_weights - row_dot)).astype(BF16)
                dk_ref[:stop] += dot(d_scores, query)
                parts.append(dot(k_t[:, :stop], d_scores))
            first = lax.broadcasted_iota(jnp.int32, parts[0].shape, 0) < HEAD_DIM
            d_query = jnp.where(first, parts[0], parts[1]).T * SCORE_SCALE
            d_query = d_query * cos_ref[rows] - turn(d_query) * sin_ref[rows]
            out_ref[rows, lanes] = d_query.astype(BF16)
    d_key = dk_ref[...]
    d_key = d_key + pltpu.roll(d_key, HEAD_DIM, 1)
    d_key = d_key * cos_ref[...] - turn(d_key) * sin_ref[...]
    d_value = dv_ref[...]
    d_value = d_value + pltpu.roll(d_value, HEAD_DIM, 1)
    out_ref[:, pairs * PAIR :] = jnp.where(
        left_lanes(d_key.shape), d_key, d_value
    ).astype(BF16)


def attend_back(saved, grad, cosine, sine, lengths):
    query, key, value, log_sums = saved
    slots, q_width = query.shape
    block = min(BLOCK, slots)
    full = pl.BlockSpec(memory_space=pltpu.VMEM)
    return pl.pallas_call(
        functools.partial(attend_back_kernel, block),
        out_shape=jax.ShapeDtypeStruct((slots, q_width + PAIR), BF16),
        in_specs=[pl.BlockSpec(memory_space=pltpu.SMEM)] + [full] * 7,
        out_specs=full,
        scratch_shapes=[pltpu.VMEM((slots, PAIR), F32)] * 2,
        compiler_params=pltpu.CompilerParams(vmem_limit_bytes=48 << 20),
        cost_estimate=pl.CostEstimate(
            flops=10 * slots * slots * q_width, bytes_accessed=12 * slots * q_width,
            transcendentals=slots * slots * q_width // HEAD_DIM,
        ),
    )(lengths, query, key, value, log_sums, grad, cosine, sine)


def flip(mask, size):
    return [(i, i ^ mask) for i in range(size)]


def send(value, mask):
    return lax.ppermute(value, "dp", flip(mask, lax.axis_size("dp")))


def other(first):
    return 3 - first


def gather_near(shard, first):
    if lax.axis_size("dp") != 4:
        return None
    return (send(shard, first), send(shard, other(first)))


def gather_far(near, first):
    return None if near is None else send(near[0], other(first))


def place(pieces, masks, axis):
    me = lax.axis_index("dp")
    whole = None
    for mask, piece in zip(masks, pieces):
        size = piece.shape[axis]
        if whole is None:
            shape = list(piece.shape)
            shape[axis] = 4 * size
            whole = jnp.zeros(shape, piece.dtype)
        whole = lax.dynamic_update_slice_in_dim(whole, piece, (me ^ mask) * size, axis)
    return whole


def gather_direct(shard, axis):
    if lax.axis_size("dp") != 4:
        return lax.all_gather(shard, "dp", axis=axis, tiled=True)
    return place((shard, send(shard, 1), send(shard, 2), send(shard, 3)), range(4), axis)


def dp_block(partial, mask, axis):
    place = lax.axis_index("dp") ^ mask
    if partial.ndim == 2:
        size = partial.shape[1] // 4
        return lax.dynamic_slice_in_dim(partial, place * size, size, 1)
    return lax.dynamic_index_in_dim(partial, place, axis, keepdims=False)


def gather_halves(shard, near):
    if lax.axis_size("dp") != 4:
        return None
    half = shard.shape[0] // 2
    if near is None:
        return tuple(send(part, mask) for mask in (1, 2) for part in (shard[:half], shard[half:]))
    return (send(near[0], 2), send(near[3], 1))


def join_halves(shard, near, far, axis):
    if near is None:
        return lax.all_gather(shard, "dp", axis=axis, tiled=True)
    pieces = (shard,) + tuple(
        jnp.concatenate(pair, axis=0) for pair in (near[:2], near[2:], far)
    )
    return place(pieces, range(4), axis)


def scatter_first(partial, axis, first):
    if lax.axis_size("dp") != 4:
        return lax.psum_scatter(
            partial.astype(BF16), "dp", scatter_dimension=axis, tiled=partial.ndim == 2
        )
    return tuple(send(dp_block(partial, mask, axis).astype(BF16), first) for mask in (3, first))


def scatter_second(partial, got, axis, first):
    if lax.axis_size("dp") != 4:
        return got.astype(F32)
    far, beside = got
    passed = dp_block(partial, other(first), axis).astype(F32) + far.astype(F32)
    last = send(passed.astype(BF16), other(first))
    own = dp_block(partial, 0, axis).astype(F32)
    return own + beside.astype(F32) + last.astype(F32)


def scatter_begin(partial, axis):
    if lax.axis_size("dp") != 4:
        return scatter_first(partial, axis, 1)
    return tuple(send(dp_block(partial, mask, axis).astype(BF16), mask) for mask in (1, 2, 3))


def scatter_end(partial, got, axis):
    if lax.axis_size("dp") != 4:
        return got.astype(F32)
    return sum((part.astype(F32) for part in got), dp_block(partial, 0, axis).astype(F32))


def scatter_direct(partial, axis):
    return scatter_end(partial, scatter_begin(partial, axis), axis)


def swap_dp(blocks):
    if lax.axis_size("dp") != 4:
        return exchange(blocks, "dp")
    parts = [dp_block(blocks, 0, 0)] + [send(dp_block(blocks, mask, 0), mask) for mask in (1, 2, 3)]
    return place([part[None] for part in parts], range(4), 0)


def exchange(blocks, axis_name):
    return lax.all_to_all(blocks, axis_name, split_axis=0, concat_axis=0, tiled=True)


def gather_seq(shard):
    return lax.all_gather(shard, "seq", axis=0, tiled=True)


def scatter_seq(partial):
    return lax.psum_scatter(
        partial.astype(BF16), "seq", scatter_dimension=0, tiled=True
    ).astype(F32)


def gate_up_kernel(me_ref, x_ref, *refs):
    pieces, (gate_ref, up_ref, *wholes, whole, sems, out_sems) = refs[:8], refs[8:]
    me = me_ref[0]
    sub, ff = pieces[0].shape[1:]
    copies = []
    for index, piece in enumerate(pieces):
        part, mask = divmod(index, 4)
        copies.append(
            pltpu.make_async_copy(piece, whole.at[part, :, me ^ mask], sems.at[index])
        )
    for copy in copies:
        copy.start()
    for copy in copies:
        copy.wait()
    writes = [
        pltpu.make_async_copy(whole.at[part], wholes[part], out_sems.at[part]) for part in range(2)
    ]
    for write in writes:
        write.start()
    depth = whole.shape[1] * whole.shape[2] * sub
    tile = min(512, ff)
    rows = min(256, x_ref.shape[0])

    @pl.loop(0, x_ref.shape[0] // rows)
    def _(step):
        span = pl.ds(pl.multiple_of(step * rows, rows), rows)
        for start in range(0, ff, tile):
            lanes = slice(start, start + tile)
            for part, out_ref in enumerate((gate_ref, up_ref)):
                out_ref[span, lanes] = dot(
                    x_ref[span, :], whole[part, :, :, :, lanes].reshape(depth, tile)
                )

    for write in writes:
        write.wait()


def gate_up_of(normed2, pieces):
    slots = normed2.shape[0]
    seqs, sub, ff = pieces[0].shape
    whole = (2, seqs, 4, sub, ff)
    full = pl.BlockSpec(memory_space=pltpu.VMEM)
    away = pl.BlockSpec(memory_space=pl.ANY)
    shape = jax.ShapeDtypeStruct
    me = lax.axis_index("dp").astype(jnp.int32).reshape(1)
    return pl.pallas_call(
        gate_up_kernel,
        out_shape=(shape((slots, ff), F32),) * 2 + (shape(whole[1:], BF16),) * 2,
        in_specs=[pl.BlockSpec(memory_space=pltpu.SMEM), full] + [away] * len(pieces),
        out_specs=(full, full, away, away),
        scratch_shapes=[
            pltpu.VMEM(whole, BF16),
            pltpu.SemaphoreType.DMA((len(pieces),)),
            pltpu.SemaphoreType.DMA((2,)),
        ],
        compiler_params=pltpu.CompilerParams(vmem_limit_bytes=56 << 20),
        cost_estimate=pl.CostEstimate(
            flops=2 * slots * normed2.shape[1] * 2 * ff,
            bytes_accessed=8 * slots * ff + 8 * ff * normed2.shape[1],
            transcendentals=0,
        ),
    )(me, normed2, *pieces)


def local(tokens, lengths, w_qkv, w_out, w_gate_up, w_down, gains, cotangent):
    tok_rows, width = tokens.shape[1:]
    seqs, ranks = lax.axis_size("seq"), lax.axis_size("dp")
    slots = tok_rows * seqs
    q_width = ATTN // seqs
    repeats = max(1, seqs // KV_HEADS)
    ff = FF // seqs
    sub = w_qkv.shape[0] // ranks

    first_slot = lax.axis_index("seq") * tok_rows
    length = lengths[0]
    valid_rows = ((first_slot + jnp.arange(tok_rows)) < length).astype(F32)[:, None]
    cosine, sine = rotary_pair(slots)

    def split_qkv(rows):
        def heads(block):
            block = block.reshape(sub, KV_HEADS, HEAD_DIM)
            return jnp.repeat(block, repeats, axis=1)

        query = rows[:, :ATTN].reshape(sub, seqs, q_width)
        joined = jnp.concatenate(
            [query, heads(rows[:, ATTN : ATTN + KV]), heads(rows[:, ATTN + KV :])], axis=2
        )
        return joined.transpose(1, 0, 2)

    def join_qkv(blocks):
        def heads(block):
            block = block.reshape(sub, KV_HEADS, repeats, HEAD_DIM)
            if repeats > 1:
                block = block.astype(F32).sum(axis=2).astype(BF16)
            return block.reshape(sub, KV)

        blocks = blocks.transpose(1, 0, 2)
        key_part = heads(blocks[:, :, q_width : q_width + HEAD_DIM])
        value_part = heads(blocks[:, :, q_width + HEAD_DIM :])
        return jnp.concatenate([blocks[:, :, :q_width].reshape(sub, ATTN), key_part, value_part], axis=1)

    all_tokens = gather_seq(tokens[0])
    qkv_rows = swap_dp(w_qkv.reshape(ranks, sub, -1)).transpose(1, 0, 2).reshape(sub, -1)
    per_block = w_gate_up.shape[1] // ff
    qkv_rows, w_gate_up = tie((qkv_rows, w_gate_up))
    gu_rows = swap_dp(
        w_gate_up.reshape(ranks, sub, per_block, ff).transpose(0, 2, 1, 3)
    ).reshape(2, seqs, sub, ff)
    def with_gains(blocks, pair):
        rows = jnp.pad(pair, ((0, 0), (0, 6), (0, blocks.shape[2] - pair.shape[2])))
        return jnp.concatenate([blocks, rows.astype(BF16)], axis=1)

    gain_rows = jnp.broadcast_to(gains.T, (seqs, 2, gains.shape[0]))
    qkv_got = exchange(with_gains(split_qkv(qkv_rows), gain_rows), "seq")
    qkv_got, gu_rows = tie((qkv_got, gu_rows))
    gu_mine = exchange(gu_rows.transpose(1, 0, 2, 3), "seq")
    qkv_mine = qkv_got[:, :sub]
    all_gains = qkv_got[:, sub : sub + 2, : gains.shape[0]].transpose(1, 0, 2)
    all_gains = all_gains.reshape(2, width).astype(F32)
    gain_first, gain_second = all_gains[0], all_gains[1]
    my_qkv = gather_direct(qkv_mine[:, None], 1).reshape(width, q_width + PAIR)
    all_tokens, my_qkv, w_out, w_down = tie((all_tokens, my_qkv, w_out, w_down))
    my_out = gather_direct(w_out, 1)
    down_near = gather_halves(w_down, None)

    x_all = all_tokens.astype(F32)
    inv_all = lax.rsqrt(jnp.mean(x_all * x_all, axis=1, keepdims=True) + EPSILON)
    normed = (x_all * inv_all * gain_first).astype(BF16)
    qkv = dot(normed, my_qkv)
    attended, *saved = attend(qkv, cosine, sine, lengths, q_width)
    attended, gu_mine, my_out, down_near = tie((attended, gu_mine, my_out, down_near))
    gate_mine, up_mine = gu_mine[:, 0], gu_mine[:, 1]
    gate_near, up_near = gather_near(gate_mine, 1), gather_near(up_mine, 2)

    x = tokens[0].astype(F32)
    branch = scatter_seq(dot(attended, my_out))
    branch, gate_near, up_near, down_near = tie((branch, gate_near, up_near, down_near))
    gate_far, up_far = gather_far(gate_near, 1), gather_far(up_near, 2)
    down_far = gather_halves(w_down, down_near)
    hidden = x + RESIDUAL_SCALE * branch
    inv_second = lax.rsqrt(jnp.mean(hidden * hidden, axis=1, keepdims=True) + EPSILON)
    unit_second = hidden * inv_second
    normed2 = gather_seq((unit_second * gain_second).astype(BF16))
    upstream = cotangent[0].astype(F32) * valid_rows
    normed2, gate_far, up_far, down_far, late_grad = tie(
        (normed2, gate_far, up_far, down_far, (RESIDUAL_SCALE * upstream).astype(BF16))
    )
    down_grad = gather_seq(late_grad)
    my_down = join_halves(w_down, down_near, down_far, 1)

    if gate_near is None:
        my_gate, my_up = (
            lax.all_gather(mine, "dp", axis=1).reshape(width, ff) for mine in (gate_mine, up_mine)
        )
        gate_vals, up_vals = dot(normed2, my_gate), dot(normed2, my_up)
    else:
        pieces = (gate_mine, *gate_near, gate_far, up_mine, up_near[1], up_near[0], up_far)
        gate_vals, up_vals, *wholes = gate_up_of(normed2, pieces)
        my_gate, my_up = (whole.reshape(width, ff) for whole in wholes)
    sigmoid_gate = jax.nn.sigmoid(gate_vals)
    mixed = (gate_vals * sigmoid_gate * up_vals).astype(BF16)
    down_sum = dot(mixed, my_down).astype(BF16)
    down_grad, down_sum = tie((down_grad, down_sum))
    down_out = scatter_seq(down_sum)
    down_partial = dot_tn(mixed, down_grad).astype(BF16)
    down_grad, down_partial = tie((down_grad, down_partial))
    down_got = scatter_begin(down_partial, 1)
    mixed_grad = dot_nt(down_grad, my_down)
    gate_grad = (
        mixed_grad * up_vals * sigmoid_gate * (1.0 + gate_vals * (1.0 - sigmoid_gate))
    ).astype(BF16)
    up_grad = (mixed_grad * gate_vals * sigmoid_gate).astype(BF16)
    normed2_sum = (dot_nt(gate_grad, my_gate) + dot_nt(up_grad, my_up)).astype(BF16)

    gate_partial = dot_tn(normed2, gate_grad).astype(BF16).reshape(seqs, ranks, sub, ff)
    up_partial = dot_tn(normed2, up_grad).astype(BF16).reshape(seqs, ranks, sub, ff)
    normed2_sum, down_out, gate_partial, up_partial, down_got = tie(
        (normed2_sum, down_out, gate_partial, up_partial, down_got)
    )
    normed2_grad = scatter_seq(normed2_sum)
    gate_got = scatter_first(gate_partial, 1, 1)
    up_got = scatter_first(up_partial, 1, 2)
    normed2_grad, gate_got, up_got = tie((normed2_grad, gate_got, up_got))

    unit_grad2 = normed2_grad * gain_second
    hidden_grad = upstream + inv_second * (
        unit_grad2 - unit_second * jnp.mean(unit_grad2 * unit_second, axis=1, keepdims=True)
    )
    gain_second_term = jnp.sum(normed2_grad * unit_second, axis=0)
    branch_grad = gather_seq((RESIDUAL_SCALE * hidden_grad).astype(BF16))
    gu_summed = jnp.stack(
        [
            scatter_second(gate_partial, gate_got, 1, 1).astype(BF16),
            scatter_second(up_partial, up_got, 1, 2).astype(BF16),
        ],
        axis=1,
    )
    gu_summed, down_partial = tie((gu_summed, down_partial))
    grad_down = scatter_end(down_partial, down_got, 1)
    branch_grad, gu_summed = tie((branch_grad, gu_summed))
    gu_blocks = exchange(gu_summed, "seq")

    attended_grad = dot_nt(branch_grad, my_out).astype(BF16)
    qkv_grad = attend_back(saved, attended_grad, cosine, sine, lengths)
    normed_partial = dot_nt(qkv_grad, my_qkv)
    qkv_partial = dot_tn(normed, qkv_grad).astype(BF16).reshape(seqs, ranks, sub, -1)
    qkv_summed = scatter_direct(qkv_partial, 1).astype(BF16)
    out_partial = dot_tn(attended, branch_grad).astype(BF16)
    unit_all = x_all * inv_all
    gain_first_term = jnp.sum(normed_partial * unit_all, axis=0)
    gains_term = jnp.stack([gain_first_term, gain_second_term]).reshape(2, seqs, -1)
    qkv_blocks = with_gains(qkv_summed, gains_term.transpose(1, 0, 2))
    grad_out = scatter_direct(out_partial, 1)
    normed_sum, gu_blocks, grad_down, qkv_blocks, grad_out = tie(
        (normed_partial.astype(BF16), gu_blocks, grad_down, qkv_blocks, grad_out)
    )
    normed_grad = scatter_seq(normed_sum)
    gu_back = swap_dp(
        gu_blocks.transpose(1, 0, 2, 3).reshape(ranks, per_block, sub, ff)
    )
    qkv_back, gu_back = tie((exchange(qkv_blocks, "seq"), gu_back))
    gain_blocks = qkv_back[:, sub : sub + 2, : gains.shape[0]]
    qkv_back = join_qkv(qkv_back[:, :sub])
    grad_qkv = (
        swap_dp(qkv_back.reshape(sub, ranks, -1).transpose(1, 0, 2))
        .reshape(w_qkv.shape)
        .astype(F32)
    )
    grad_gate_up = gu_back.transpose(0, 2, 1, 3).reshape(w_gate_up.shape).astype(F32)

    grad_gains = jnp.sum(gain_blocks.astype(F32), axis=0)
    if ranks == 4:
        grad_gains = grad_gains + send(grad_gains, 1)
        grad_gains = (grad_gains + send(grad_gains, 2)).T
    else:
        grad_gains = lax.psum(grad_gains, "dp").T

    normed_grad, grad_qkv, grad_out, grad_gate_up, grad_gains = tie(
        (normed_grad, grad_qkv, grad_out, grad_gate_up, grad_gains)
    )
    output = (valid_rows * (hidden + RESIDUAL_SCALE * down_out)).astype(BF16)
    inv_first = lax.rsqrt(jnp.mean(x * x, axis=1, keepdims=True) + EPSILON)
    unit_first = x * inv_first
    unit_grad1 = normed_grad * gain_first
    token_grad = hidden_grad + inv_first * (
        unit_grad1 - unit_first * jnp.mean(unit_grad1 * unit_first, axis=1, keepdims=True)
    )
    return (output[None], token_grad[None], grad_qkv, grad_out, grad_gate_up, grad_down, grad_gains)


def solution(mesh):
    in_specs = (
        P("dp", "seq", None),
        P("dp"),
        P("seq", "dp"),
        P("seq", "dp"),
        P("seq", "dp"),
        P("seq", "dp"),
        P("seq", None),
        P("dp", "seq", None),
    )
    out_specs = (
        P("dp", "seq", None),
        P("dp", "seq", None),
        P("seq", "dp"),
        P("seq", "dp"),
        P("seq", "dp"),
        P("seq", "dp"),
        P("seq", None),
    )
    return jax.shard_map(local, mesh=mesh, in_specs=in_specs, out_specs=out_specs, check_vma=False)
```

```python
import functools

import jax
import jax.numpy as jnp
from jax import lax
from jax.experimental import pallas as pl
from jax.experimental.pallas import tpu as pltpu
from jax.sharding import PartitionSpec as P

HEADS = 32
KV_HEADS = 8
HEAD_DIM = 64
FF = 8192
ATTN = HEADS * HEAD_DIM
KV = KV_HEADS * HEAD_DIM
PAIR = 2 * HEAD_DIM

EPSILON = 1e-05
RESIDUAL_SCALE = 0.22
SCORE_SCALE = 1.0 / 64.0
ROPE_THETA = 10000000.0
BLOCK = 256

BF16 = jnp.bfloat16
F32 = jnp.float32


def dot(left, right):
    return jnp.dot(left, right, preferred_element_type=F32)


def dot_nt(left, right):
    return lax.dot_general(left, right, (((1,), (1,)), ((), ())), preferred_element_type=F32)


def dot_tn(left, right):
    return lax.dot_general(left, right, (((0,), (0,)), ((), ())), preferred_element_type=F32)


tie = lax.optimization_barrier


def rotary_pair(slots):
    half_dim = HEAD_DIM // 2
    frequency = ROPE_THETA ** (-(jnp.arange(half_dim, dtype=F32) * 2.0) / HEAD_DIM)
    angles = jnp.arange(slots, dtype=jnp.int32).astype(F32)[:, None] * frequency[None, :]
    angles = jnp.concatenate([angles] * 4, axis=1)
    return (jnp.cos(angles), jnp.sin(angles))


def turn(values):
    half = HEAD_DIM // 2
    lane = lax.broadcasted_iota(jnp.int32, values.shape, 1) % HEAD_DIM
    ahead = pltpu.roll(values, PAIR - half, 1)
    behind = pltpu.roll(values, half, 1)
    return jnp.where(lane < half, -ahead, behind)


def left_lanes(shape):
    return lax.broadcasted_iota(jnp.int32, shape, 1) < HEAD_DIM


def mask_bias(start, block, stop, length):
    key = lax.broadcasted_iota(jnp.int32, (stop, block), 0)
    query = lax.broadcasted_iota(jnp.int32, (stop, block), 1) + start
    return jnp.where((key <= query) & (key < length), 0.0, -1e30)


def attend_kernel(block, length_ref, qkv_ref, cos_ref, sin_ref, out_ref, q_ref, k_ref, v_ref, lse_ref):
    slots = qkv_ref.shape[0]
    pairs = q_ref.shape[1] // PAIR
    length = length_ref[0]
    cosine, sine = cos_ref[...], sin_ref[...]
    for pair in range(pairs):
        lanes = slice(pair * PAIR, (pair + 1) * PAIR)
        values = qkv_ref[:, lanes]
        rotated = (values * cosine + turn(values) * sine).astype(BF16)
        q_ref[:, lanes] = rotated * jnp.asarray(SCORE_SCALE, BF16)
    values = qkv_ref[:, pairs * PAIR :]
    left = left_lanes(values.shape)
    swapped = pltpu.roll(values, HEAD_DIM, 1)
    keys = jnp.where(left, values, swapped)
    k_ref[...] = (keys * cosine + turn(keys) * sine).astype(BF16)
    v_both = jnp.where(left, swapped, values)
    v_ref[...] = v_both.astype(BF16)
    v_t = v_both.T.astype(BF16)
    lse_ref[...] = jnp.zeros_like(lse_ref)
    for start in range(0, slots, block):
        stop = start + block
        rows = slice(start, stop)
        bias = mask_bias(start, block, stop, length)
        keys = k_ref[:stop]
        for pair in range(pairs):
            lanes = slice(pair * PAIR, (pair + 1) * PAIR)
            queries = q_ref[rows, lanes]
            left = left_lanes(queries.shape)
            outs = []
            for side in range(2):
                query = jnp.where(left == (side == 0), queries, jnp.zeros_like(queries))
                scores = dot_nt(keys, query) + bias
                largest = jnp.max(scores, axis=0, keepdims=True)
                weights = jnp.exp(scores - largest)
                total = jnp.sum(weights, axis=0, keepdims=True)
                head = 2 * pair + side
                lse_ref[head : head + 1, rows] = largest + jnp.log(total)
                probabilities = (weights * (1.0 / total)).astype(BF16)
                outs.append(dot(v_t[:, :stop], probabilities))
            first = lax.broadcasted_iota(jnp.int32, outs[0].shape, 0) < HEAD_DIM
            out_ref[rows, lanes] = jnp.where(first, outs[0], outs[1]).T.astype(BF16)


def attend(qkv, cosine, sine, lengths, q_width):
    slots = qkv.shape[0]
    block = min(BLOCK, slots)
    full = pl.BlockSpec(memory_space=pltpu.VMEM)
    shape = jax.ShapeDtypeStruct
    return pl.pallas_call(
        functools.partial(attend_kernel, block),
        out_shape=(
            shape((slots, q_width), BF16),
            shape((slots, q_width), BF16),
            shape((slots, PAIR), BF16),
            shape((slots, PAIR), BF16),
            shape((8, slots), F32),
        ),
        in_specs=[pl.BlockSpec(memory_space=pltpu.SMEM), full, full, full],
        out_specs=(full,) * 5,
        compiler_params=pltpu.CompilerParams(vmem_limit_bytes=48 << 20),
        cost_estimate=pl.CostEstimate(
            flops=4 * slots * slots * q_width, bytes_accessed=12 * slots * q_width,
            transcendentals=slots * slots * q_width // HEAD_DIM,
        ),
    )(lengths, qkv, cosine, sine)


def attend_back_kernel(
    block, length_ref, q_ref, k_ref, v_ref, lse_ref, grad_ref, cos_ref, sin_ref, out_ref, dk_ref, dv_ref
):
    slots = q_ref.shape[0]
    pairs = q_ref.shape[1] // PAIR
    length = length_ref[0]
    dk_ref[...] = jnp.zeros_like(dk_ref)
    dv_ref[...] = jnp.zeros_like(dv_ref)
    k_t = k_ref[...].astype(F32).T.astype(BF16)
    for start in range(0, slots, block):
        stop = start + block
        rows = slice(start, stop)
        bias = mask_bias(start, block, stop, length)
        keys, values = k_ref[:stop], v_ref[:stop]
        for pair in range(pairs):
            lanes = slice(pair * PAIR, (pair + 1) * PAIR)
            queries, grads = q_ref[rows, lanes], grad_ref[rows, lanes]
            left = left_lanes(queries.shape)
            parts = []
            for side in range(2):
                head = 2 * pair + side
                query = jnp.where(left == (side == 0), queries, jnp.zeros_like(queries))
                grad = jnp.where(left == (side == 0), grads, jnp.zeros_like(grads))
                scores = dot_nt(keys, query) + bias
                weights = jnp.exp(scores - lse_ref[head : head + 1, rows])
                dv_ref[:stop] += dot(weights.astype(BF16), grad)
                d_weights = dot_nt(values, grad)
                row_dot = jnp.sum(weights * d_weights, axis=0, keepdims=True)
                d_scores = (weights * (d_weights - row_dot)).astype(BF16)
                dk_ref[:stop] += dot(d_scores, query)
                parts.append(dot(k_t[:, :stop], d_scores))
            first = lax.broadcasted_iota(jnp.int32, parts[0].shape, 0) < HEAD_DIM
            d_query = jnp.where(first, parts[0], parts[1]).T * SCORE_SCALE
            d_query = d_query * cos_ref[rows] - turn(d_query) * sin_ref[rows]
            out_ref[rows, lanes] = d_query.astype(BF16)
    d_key = dk_ref[...]
    d_key = d_key + pltpu.roll(d_key, HEAD_DIM, 1)
    d_key = d_key * cos_ref[...] - turn(d_key) * sin_ref[...]
    d_value = dv_ref[...]
    d_value = d_value + pltpu.roll(d_value, HEAD_DIM, 1)
    out_ref[:, pairs * PAIR :] = jnp.where(
        left_lanes(d_key.shape), d_key, d_value
    ).astype(BF16)


def attend_back(saved, grad, cosine, sine, lengths):
    query, key, value, log_sums = saved
    slots, q_width = query.shape
    block = min(BLOCK, slots)
    full = pl.BlockSpec(memory_space=pltpu.VMEM)
    return pl.pallas_call(
        functools.partial(attend_back_kernel, block),
        out_shape=jax.ShapeDtypeStruct((slots, q_width + PAIR), BF16),
        in_specs=[pl.BlockSpec(memory_space=pltpu.SMEM)] + [full] * 7,
        out_specs=full,
        scratch_shapes=[pltpu.VMEM((slots, PAIR), F32)] * 2,
        compiler_params=pltpu.CompilerParams(vmem_limit_bytes=48 << 20),
        cost_estimate=pl.CostEstimate(
            flops=10 * slots * slots * q_width, bytes_accessed=12 * slots * q_width,
            transcendentals=slots * slots * q_width // HEAD_DIM,
        ),
    )(lengths, query, key, value, log_sums, grad, cosine, sine)


def flip(mask, size):
    return [(i, i ^ mask) for i in range(size)]


def send(value, mask):
    return lax.ppermute(value, "dp", flip(mask, lax.axis_size("dp")))


def other(first):
    return 3 - first


def gather_near(shard, first):
    if lax.axis_size("dp") != 4:
        return None
    return (send(shard, first), send(shard, other(first)))


def gather_far(near, first):
    return None if near is None else send(near[0], other(first))


def place(pieces, masks, axis):
    me = lax.axis_index("dp")
    whole = None
    for mask, piece in zip(masks, pieces):
        size = piece.shape[axis]
        if whole is None:
            shape = list(piece.shape)
            shape[axis] = 4 * size
            whole = jnp.zeros(shape, piece.dtype)
        whole = lax.dynamic_update_slice_in_dim(whole, piece, (me ^ mask) * size, axis)
    return whole


def gather_direct(shard, axis):
    if lax.axis_size("dp") != 4:
        return lax.all_gather(shard, "dp", axis=axis, tiled=True)
    return place((shard, send(shard, 1), send(shard, 2), send(shard, 3)), range(4), axis)


def dp_block(partial, mask, axis):
    place = lax.axis_index("dp") ^ mask
    if partial.ndim == 2:
        size = partial.shape[1] // 4
        return lax.dynamic_slice_in_dim(partial, place * size, size, 1)
    return lax.dynamic_index_in_dim(partial, place, axis, keepdims=False)


def gather_halves(shard, near):
    if lax.axis_size("dp") != 4:
        return None
    half = shard.shape[0] // 2
    if near is None:
        return tuple(send(part, mask) for mask in (1, 2) for part in (shard[:half], shard[half:]))
    return (send(near[0], 2), send(near[3], 1))


def join_halves(shard, near, far, axis):
    if near is None:
        return lax.all_gather(shard, "dp", axis=axis, tiled=True)
    pieces = (shard,) + tuple(
        jnp.concatenate(pair, axis=0) for pair in (near[:2], near[2:], far)
    )
    return place(pieces, range(4), axis)


def scatter_first(partial, axis, first):
    if lax.axis_size("dp") != 4:
        return lax.psum_scatter(
            partial.astype(BF16), "dp", scatter_dimension=axis, tiled=partial.ndim == 2
        )
    return tuple(send(dp_block(partial, mask, axis).astype(BF16), first) for mask in (3, first))


def scatter_second(partial, got, axis, first):
    if lax.axis_size("dp") != 4:
        return got.astype(F32)
    far, beside = got
    passed = dp_block(partial, other(first), axis).astype(F32) + far.astype(F32)
    last = send(passed.astype(BF16), other(first))
    own = dp_block(partial, 0, axis).astype(F32)
    return own + beside.astype(F32) + last.astype(F32)


def scatter_begin(partial, axis):
    if lax.axis_size("dp") != 4:
        return scatter_first(partial, axis, 1)
    return tuple(send(dp_block(partial, mask, axis).astype(BF16), mask) for mask in (1, 2, 3))


def scatter_end(partial, got, axis):
    if lax.axis_size("dp") != 4:
        return got.astype(F32)
    return sum((part.astype(F32) for part in got), dp_block(partial, 0, axis).astype(F32))


def scatter_halves(partial):
    if lax.axis_size("dp") != 4:
        return scatter_first(partial, 1, 1)
    half = partial.shape[0] // 2
    beside, across, far = (dp_block(partial, mask, 1) for mask in (1, 2, 3))
    top = jnp.stack([beside[:half], far[:half]])
    low = jnp.stack([across[half:], far[half:]])
    return (send(top, 1), send(low, 2))


def halves_next(partial, got):
    if lax.axis_size("dp") != 4:
        return got
    half = partial.shape[0] // 2
    beside, across = (dp_block(partial, mask, 1).astype(F32) for mask in (1, 2))
    top, low = (part[1].astype(F32) for part in got)
    return (
        send((across[:half] + top).astype(BF16), 2),
        send((beside[half:] + low).astype(BF16), 1),
    )


def halves_end(partial, got, last):
    if lax.axis_size("dp") != 4:
        return got.astype(F32)
    half = partial.shape[0] // 2
    own = dp_block(partial, 0, 1).astype(F32)
    sums = [
        rows + first[0].astype(F32) + second.astype(F32)
        for rows, first, second in zip((own[:half], own[half:]), got, last)
    ]
    return jnp.concatenate(sums, axis=0)


def scatter_direct(partial, axis):
    return scatter_end(partial, scatter_begin(partial, axis), axis)


def swap_dp(blocks):
    if lax.axis_size("dp") != 4:
        return exchange(blocks, "dp")
    parts = [dp_block(blocks, 0, 0)] + [send(dp_block(blocks, mask, 0), mask) for mask in (1, 2, 3)]
    return place([part[None] for part in parts], range(4), 0)


def exchange(blocks, axis_name):
    return lax.all_to_all(blocks, axis_name, split_axis=0, concat_axis=0, tiled=True)


def gather_seq(shard):
    return lax.all_gather(shard, "seq", axis=0, tiled=True)


def scatter_seq(partial):
    return lax.psum_scatter(
        partial.astype(BF16), "seq", scatter_dimension=0, tiled=True
    ).astype(F32)


def gate_up_kernel(me_ref, x_ref, *refs):
    pieces, (gate_ref, up_ref, *wholes, whole, sems, out_sems) = refs[:8], refs[8:]
    me = me_ref[0]
    sub, ff = pieces[0].shape[1:]
    copies = []
    for index, piece in enumerate(pieces):
        part, mask = divmod(index, 4)
        copies.append(
            pltpu.make_async_copy(piece, whole.at[part, :, me ^ mask], sems.at[index])
        )
    for copy in copies:
        copy.start()
    for copy in copies:
        copy.wait()
    writes = [
        pltpu.make_async_copy(whole.at[part], wholes[part], out_sems.at[part]) for part in range(2)
    ]
    for write in writes:
        write.start()
    depth = whole.shape[1] * whole.shape[2] * sub
    tile = min(512, ff)
    rows = min(256, x_ref.shape[0])

    @pl.loop(0, x_ref.shape[0] // rows)
    def _(step):
        span = pl.ds(pl.multiple_of(step * rows, rows), rows)
        for start in range(0, ff, tile):
            lanes = slice(start, start + tile)
            for part, out_ref in enumerate((gate_ref, up_ref)):
                out_ref[span, lanes] = dot(
                    x_ref[span, :], whole[part, :, :, :, lanes].reshape(depth, tile)
                )

    for write in writes:
        write.wait()


def gate_up_of(normed2, pieces):
    slots = normed2.shape[0]
    seqs, sub, ff = pieces[0].shape
    whole = (2, seqs, 4, sub, ff)
    full = pl.BlockSpec(memory_space=pltpu.VMEM)
    away = pl.BlockSpec(memory_space=pl.ANY)
    shape = jax.ShapeDtypeStruct
    me = lax.axis_index("dp").astype(jnp.int32).reshape(1)
    return pl.pallas_call(
        gate_up_kernel,
        out_shape=(shape((slots, ff), F32),) * 2 + (shape(whole[1:], BF16),) * 2,
        in_specs=[pl.BlockSpec(memory_space=pltpu.SMEM), full] + [away] * len(pieces),
        out_specs=(full, full, away, away),
        scratch_shapes=[
            pltpu.VMEM(whole, BF16),
            pltpu.SemaphoreType.DMA((len(pieces),)),
            pltpu.SemaphoreType.DMA((2,)),
        ],
        compiler_params=pltpu.CompilerParams(vmem_limit_bytes=56 << 20),
        cost_estimate=pl.CostEstimate(
            flops=2 * slots * normed2.shape[1] * 2 * ff,
            bytes_accessed=8 * slots * ff + 8 * ff * normed2.shape[1],
            transcendentals=0,
        ),
    )(me, normed2, *pieces)


def local(tokens, lengths, w_qkv, w_out, w_gate_up, w_down, gains, cotangent):
    tok_rows, width = tokens.shape[1:]
    seqs, ranks = lax.axis_size("seq"), lax.axis_size("dp")
    slots = tok_rows * seqs
    q_width = ATTN // seqs
    repeats = max(1, seqs // KV_HEADS)
    ff = FF // seqs
    sub = w_qkv.shape[0] // ranks

    first_slot = lax.axis_index("seq") * tok_rows
    length = lengths[0]
    valid_rows = ((first_slot + jnp.arange(tok_rows)) < length).astype(F32)[:, None]
    cosine, sine = rotary_pair(slots)

    def split_qkv(rows):
        def heads(block):
            block = block.reshape(sub, KV_HEADS, HEAD_DIM)
            return jnp.repeat(block, repeats, axis=1)

        query = rows[:, :ATTN].reshape(sub, seqs, q_width)
        joined = jnp.concatenate(
            [query, heads(rows[:, ATTN : ATTN + KV]), heads(rows[:, ATTN + KV :])], axis=2
        )
        return joined.transpose(1, 0, 2)

    def join_qkv(blocks):
        def heads(block):
            block = block.reshape(sub, KV_HEADS, repeats, HEAD_DIM)
            if repeats > 1:
                block = block.astype(F32).sum(axis=2).astype(BF16)
            return block.reshape(sub, KV)

        blocks = blocks.transpose(1, 0, 2)
        key_part = heads(blocks[:, :, q_width : q_width + HEAD_DIM])
        value_part = heads(blocks[:, :, q_width + HEAD_DIM :])
        return jnp.concatenate([blocks[:, :, :q_width].reshape(sub, ATTN), key_part, value_part], axis=1)

    all_tokens = gather_seq(tokens[0])
    qkv_rows = swap_dp(w_qkv.reshape(ranks, sub, -1)).transpose(1, 0, 2).reshape(sub, -1)
    per_block = w_gate_up.shape[1] // ff
    qkv_rows, w_gate_up = tie((qkv_rows, w_gate_up))
    gu_rows = swap_dp(
        w_gate_up.reshape(ranks, sub, per_block, ff).transpose(0, 2, 1, 3)
    ).reshape(2, seqs, sub, ff)
    def with_gains(blocks, pair):
        rows = jnp.pad(pair, ((0, 0), (0, 6), (0, blocks.shape[2] - pair.shape[2])))
        return jnp.concatenate([blocks, rows.astype(BF16)], axis=1)

    gain_rows = jnp.broadcast_to(gains.T, (seqs, 2, gains.shape[0]))
    qkv_got = exchange(with_gains(split_qkv(qkv_rows), gain_rows), "seq")
    qkv_got, gu_rows = tie((qkv_got, gu_rows))
    gu_mine = exchange(gu_rows.transpose(1, 0, 2, 3), "seq")
    qkv_mine = qkv_got[:, :sub]
    all_gains = qkv_got[:, sub : sub + 2, : gains.shape[0]].transpose(1, 0, 2)
    all_gains = all_gains.reshape(2, width).astype(F32)
    gain_first, gain_second = all_gains[0], all_gains[1]
    my_qkv = gather_direct(qkv_mine[:, None], 1).reshape(width, q_width + PAIR)
    all_tokens, my_qkv, w_out, w_down = tie((all_tokens, my_qkv, w_out, w_down))
    my_out = gather_direct(w_out, 1)
    down_near = gather_halves(w_down, None)

    x_all = all_tokens.astype(F32)
    inv_all = lax.rsqrt(jnp.mean(x_all * x_all, axis=1, keepdims=True) + EPSILON)
    normed = (x_all * inv_all * gain_first).astype(BF16)
    qkv = dot(normed, my_qkv)
    attended, *saved = attend(qkv, cosine, sine, lengths, q_width)
    attended, gu_mine, my_out, down_near = tie((attended, gu_mine, my_out, down_near))
    gate_mine, up_mine = gu_mine[:, 0], gu_mine[:, 1]
    gate_near, up_near = gather_near(gate_mine, 1), gather_near(up_mine, 2)

    x = tokens[0].astype(F32)
    branch = scatter_seq(dot(attended, my_out))
    branch, gate_near, up_near, down_near = tie((branch, gate_near, up_near, down_near))
    gate_far, up_far = gather_far(gate_near, 1), gather_far(up_near, 2)
    down_far = gather_halves(w_down, down_near)
    hidden = x + RESIDUAL_SCALE * branch
    inv_second = lax.rsqrt(jnp.mean(hidden * hidden, axis=1, keepdims=True) + EPSILON)
    unit_second = hidden * inv_second
    normed2 = gather_seq((unit_second * gain_second).astype(BF16))
    upstream = cotangent[0].astype(F32) * valid_rows
    normed2, gate_far, up_far, down_far, late_grad = tie(
        (normed2, gate_far, up_far, down_far, (RESIDUAL_SCALE * upstream).astype(BF16))
    )
    down_grad = gather_seq(late_grad)
    my_down = join_halves(w_down, down_near, down_far, 1)

    if gate_near is None:
        my_gate, my_up = (
            lax.all_gather(mine, "dp", axis=1).reshape(width, ff) for mine in (gate_mine, up_mine)
        )
        gate_vals, up_vals = dot(normed2, my_gate), dot(normed2, my_up)
    else:
        pieces = (gate_mine, *gate_near, gate_far, up_mine, up_near[1], up_near[0], up_far)
        gate_vals, up_vals, *wholes = gate_up_of(normed2, pieces)
        my_gate, my_up = (whole.reshape(width, ff) for whole in wholes)
    sigmoid_gate = jax.nn.sigmoid(gate_vals)
    mixed = (gate_vals * sigmoid_gate * up_vals).astype(BF16)
    down_sum = dot(mixed, my_down).astype(BF16)
    down_grad, down_sum = tie((down_grad, down_sum))
    down_out = scatter_seq(down_sum)
    down_partial = dot_tn(mixed, down_grad).astype(BF16)
    down_grad, down_partial = tie((down_grad, down_partial))
    down_got = scatter_halves(down_partial)
    mixed_grad = dot_nt(down_grad, my_down)
    gate_grad = (
        mixed_grad * up_vals * sigmoid_gate * (1.0 + gate_vals * (1.0 - sigmoid_gate))
    ).astype(BF16)
    up_grad = (mixed_grad * gate_vals * sigmoid_gate).astype(BF16)
    normed2_sum = (dot_nt(gate_grad, my_gate) + dot_nt(up_grad, my_up)).astype(BF16)

    gate_partial = dot_tn(normed2, gate_grad).astype(BF16).reshape(seqs, ranks, sub, ff)
    up_partial = dot_tn(normed2, up_grad).astype(BF16).reshape(seqs, ranks, sub, ff)
    normed2_sum, down_out, gate_partial, up_partial, down_got = tie(
        (normed2_sum, down_out, gate_partial, up_partial, down_got)
    )
    normed2_grad = scatter_seq(normed2_sum)
    gate_got = scatter_first(gate_partial, 1, 1)
    up_got = scatter_first(up_partial, 1, 2)
    normed2_grad, gate_got, up_got = tie((normed2_grad, gate_got, up_got))

    unit_grad2 = normed2_grad * gain_second
    hidden_grad = upstream + inv_second * (
        unit_grad2 - unit_second * jnp.mean(unit_grad2 * unit_second, axis=1, keepdims=True)
    )
    gain_second_term = jnp.sum(normed2_grad * unit_second, axis=0)
    branch_grad = gather_seq((RESIDUAL_SCALE * hidden_grad).astype(BF16))
    gu_summed = jnp.stack(
        [
            scatter_second(gate_partial, gate_got, 1, 1).astype(BF16),
            scatter_second(up_partial, up_got, 1, 2).astype(BF16),
        ],
        axis=1,
    )
    down_last = halves_next(down_partial, down_got)
    gu_summed, down_last = tie((gu_summed, down_last))
    branch_grad, gu_summed = tie((branch_grad, gu_summed))
    gu_blocks = exchange(gu_summed, "seq")

    out_partial = dot_tn(attended, branch_grad).astype(BF16)
    attended_grad = dot_nt(branch_grad, my_out).astype(BF16)
    attended_grad, out_partial = tie((attended_grad, out_partial))
    out_got = scatter_begin(out_partial, 1)
    qkv_grad = attend_back(saved, attended_grad, cosine, sine, lengths)
    qkv_grad, down_last = tie((qkv_grad, down_last))
    grad_down = halves_end(down_partial, down_got, down_last)
    qkv_partial = dot_tn(normed, qkv_grad).astype(BF16).reshape(seqs, ranks, sub, -1)
    qkv_partial, qkv_grad = tie((qkv_partial, qkv_grad))
    qkv_summed = scatter_direct(qkv_partial, 1).astype(BF16)
    normed_partial = dot_nt(qkv_grad, my_qkv)
    unit_all = x_all * inv_all
    gain_first_term = jnp.sum(normed_partial * unit_all, axis=0)
    gains_term = jnp.stack([gain_first_term, gain_second_term]).reshape(2, seqs, -1)
    qkv_blocks = with_gains(qkv_summed, gains_term.transpose(1, 0, 2))
    grad_out = scatter_end(out_partial, out_got, 1)
    normed_sum, gu_blocks, grad_down, qkv_blocks, grad_out = tie(
        (normed_partial.astype(BF16), gu_blocks, grad_down, qkv_blocks, grad_out)
    )
    normed_grad = scatter_seq(normed_sum)
    gu_back = swap_dp(
        gu_blocks.transpose(1, 0, 2, 3).reshape(ranks, per_block, sub, ff)
    )
    qkv_back, gu_back = tie((exchange(qkv_blocks, "seq"), gu_back))
    gain_blocks = qkv_back[:, sub : sub + 2, : gains.shape[0]]
    qkv_back = join_qkv(qkv_back[:, :sub])
    grad_qkv = (
        swap_dp(qkv_back.reshape(sub, ranks, -1).transpose(1, 0, 2))
        .reshape(w_qkv.shape)
        .astype(F32)
    )
    grad_gate_up = gu_back.transpose(0, 2, 1, 3).reshape(w_gate_up.shape).astype(F32)

    grad_gains = jnp.sum(gain_blocks.astype(F32), axis=0)
    if ranks == 4:
        grad_gains = grad_gains + send(grad_gains, 1)
        grad_gains = (grad_gains + send(grad_gains, 2)).T
    else:
        grad_gains = lax.psum(grad_gains, "dp").T

    normed_grad, grad_qkv, grad_out, grad_gate_up, grad_gains = tie(
        (normed_grad, grad_qkv, grad_out, grad_gate_up, grad_gains)
    )
    output = (valid_rows * (hidden + RESIDUAL_SCALE * down_out)).astype(BF16)
    inv_first = lax.rsqrt(jnp.mean(x * x, axis=1, keepdims=True) + EPSILON)
    unit_first = x * inv_first
    unit_grad1 = normed_grad * gain_first
    token_grad = hidden_grad + inv_first * (
        unit_grad1 - unit_first * jnp.mean(unit_grad1 * unit_first, axis=1, keepdims=True)
    )
    return (output[None], token_grad[None], grad_qkv, grad_out, grad_gate_up, grad_down, grad_gains)


def solution(mesh):
    in_specs = (
        P("dp", "seq", None),
        P("dp"),
        P("seq", "dp"),
        P("seq", "dp"),
        P("seq", "dp"),
        P("seq", "dp"),
        P("seq", None),
        P("dp", "seq", None),
    )
    out_specs = (
        P("dp", "seq", None),
        P("dp", "seq", None),
        P("seq", "dp"),
        P("seq", "dp"),
        P("seq", "dp"),
        P("seq", "dp"),
        P("seq", None),
    )
    return jax.shard_map(local, mesh=mesh, in_specs=in_specs, out_specs=out_specs, check_vma=False)
```

```python
import functools

import jax
import jax.numpy as jnp
from jax import lax
from jax.experimental import pallas as pl
from jax.experimental.pallas import tpu as pltpu
from jax.sharding import PartitionSpec as P

HEADS = 32
KV_HEADS = 8
HEAD_DIM = 64
FF = 8192
ATTN = HEADS * HEAD_DIM
KV = KV_HEADS * HEAD_DIM
PAIR = 2 * HEAD_DIM

EPSILON = 1e-05
RESIDUAL_SCALE = 0.22
SCORE_SCALE = 1.0 / 64.0
ROPE_THETA = 10000000.0
BLOCK = 256

BF16 = jnp.bfloat16
F32 = jnp.float32


def dot(left, right):
    return jnp.dot(left, right, preferred_element_type=F32)


def dot_nt(left, right):
    return lax.dot_general(left, right, (((1,), (1,)), ((), ())), preferred_element_type=F32)


def dot_tn(left, right):
    return lax.dot_general(left, right, (((0,), (0,)), ((), ())), preferred_element_type=F32)


tie = lax.optimization_barrier


def rotary_pair(slots):
    half_dim = HEAD_DIM // 2
    frequency = ROPE_THETA ** (-(jnp.arange(half_dim, dtype=F32) * 2.0) / HEAD_DIM)
    angles = jnp.arange(slots, dtype=jnp.int32).astype(F32)[:, None] * frequency[None, :]
    angles = jnp.concatenate([angles] * 4, axis=1)
    return (jnp.cos(angles), jnp.sin(angles))


def turn(values):
    half = HEAD_DIM // 2
    lane = lax.broadcasted_iota(jnp.int32, values.shape, 1) % HEAD_DIM
    ahead = pltpu.roll(values, PAIR - half, 1)
    behind = pltpu.roll(values, half, 1)
    return jnp.where(lane < half, -ahead, behind)


def left_lanes(shape):
    return lax.broadcasted_iota(jnp.int32, shape, 1) < HEAD_DIM


def mask_bias(start, block, stop, length):
    key = lax.broadcasted_iota(jnp.int32, (stop, block), 0)
    query = lax.broadcasted_iota(jnp.int32, (stop, block), 1) + start
    return jnp.where((key <= query) & (key < length), 0.0, -1e30)


def attend_kernel(block, length_ref, qkv_ref, cos_ref, sin_ref, out_ref, q_ref, k_ref, v_ref, lse_ref):
    slots = qkv_ref.shape[0]
    pairs = q_ref.shape[1] // PAIR
    length = length_ref[0]
    cosine, sine = cos_ref[...], sin_ref[...]
    for pair in range(pairs):
        lanes = slice(pair * PAIR, (pair + 1) * PAIR)
        values = qkv_ref[:, lanes]
        rotated = (values * cosine + turn(values) * sine).astype(BF16)
        q_ref[:, lanes] = rotated * jnp.asarray(SCORE_SCALE, BF16)
    values = qkv_ref[:, pairs * PAIR :]
    left = left_lanes(values.shape)
    swapped = pltpu.roll(values, HEAD_DIM, 1)
    keys = jnp.where(left, values, swapped)
    k_ref[...] = (keys * cosine + turn(keys) * sine).astype(BF16)
    v_both = jnp.where(left, swapped, values)
    v_ref[...] = v_both.astype(BF16)
    v_t = v_both.T.astype(BF16)
    lse_ref[...] = jnp.zeros_like(lse_ref)
    for start in range(0, slots, block):
        stop = start + block
        rows = slice(start, stop)
        bias = mask_bias(start, block, stop, length)
        keys = k_ref[:stop]
        for pair in range(pairs):
            lanes = slice(pair * PAIR, (pair + 1) * PAIR)
            queries = q_ref[rows, lanes]
            left = left_lanes(queries.shape)
            outs = []
            for side in range(2):
                query = jnp.where(left == (side == 0), queries, jnp.zeros_like(queries))
                scores = dot_nt(keys, query) + bias
                largest = jnp.max(scores, axis=0, keepdims=True)
                weights = jnp.exp(scores - largest)
                total = jnp.sum(weights, axis=0, keepdims=True)
                head = 2 * pair + side
                lse_ref[head : head + 1, rows] = largest + jnp.log(total)
                probabilities = (weights * (1.0 / total)).astype(BF16)
                outs.append(dot(v_t[:, :stop], probabilities))
            first = lax.broadcasted_iota(jnp.int32, outs[0].shape, 0) < HEAD_DIM
            out_ref[rows, lanes] = jnp.where(first, outs[0], outs[1]).T.astype(BF16)


def attend(qkv, cosine, sine, lengths, q_width):
    slots = qkv.shape[0]
    block = min(BLOCK, slots)
    full = pl.BlockSpec(memory_space=pltpu.VMEM)
    shape = jax.ShapeDtypeStruct
    return pl.pallas_call(
        functools.partial(attend_kernel, block),
        out_shape=(
            shape((slots, q_width), BF16),
            shape((slots, q_width), BF16),
            shape((slots, PAIR), BF16),
            shape((slots, PAIR), BF16),
            shape((8, slots), F32),
        ),
        in_specs=[pl.BlockSpec(memory_space=pltpu.SMEM), full, full, full],
        out_specs=(full,) * 5,
        compiler_params=pltpu.CompilerParams(vmem_limit_bytes=48 << 20),
        cost_estimate=pl.CostEstimate(
            flops=4 * slots * slots * q_width, bytes_accessed=12 * slots * q_width,
            transcendentals=slots * slots * q_width // HEAD_DIM,
        ),
    )(lengths, qkv, cosine, sine)


def attend_back_kernel(
    block, length_ref, q_ref, k_ref, v_ref, lse_ref, grad_ref, cos_ref, sin_ref, out_ref, dk_ref, dv_ref
):
    slots = q_ref.shape[0]
    pairs = q_ref.shape[1] // PAIR
    length = length_ref[0]
    dk_ref[...] = jnp.zeros_like(dk_ref)
    dv_ref[...] = jnp.zeros_like(dv_ref)
    k_t = k_ref[...].astype(F32).T.astype(BF16)
    for start in range(0, slots, block):
        stop = start + block
        rows = slice(start, stop)
        bias = mask_bias(start, block, stop, length)
        keys, values = k_ref[:stop], v_ref[:stop]
        for pair in range(pairs):
            lanes = slice(pair * PAIR, (pair + 1) * PAIR)
            queries, grads = q_ref[rows, lanes], grad_ref[rows, lanes]
            left = left_lanes(queries.shape)
            parts = []
            for side in range(2):
                head = 2 * pair + side
                query = jnp.where(left == (side == 0), queries, jnp.zeros_like(queries))
                grad = jnp.where(left == (side == 0), grads, jnp.zeros_like(grads))
                scores = dot_nt(keys, query) + bias
                weights = jnp.exp(scores - lse_ref[head : head + 1, rows])
                dv_ref[:stop] += dot(weights.astype(BF16), grad)
                d_weights = dot_nt(values, grad)
                row_dot = jnp.sum(weights * d_weights, axis=0, keepdims=True)
                d_scores = (weights * (d_weights - row_dot)).astype(BF16)
                dk_ref[:stop] += dot(d_scores, query)
                parts.append(dot(k_t[:, :stop], d_scores))
            first = lax.broadcasted_iota(jnp.int32, parts[0].shape, 0) < HEAD_DIM
            d_query = jnp.where(first, parts[0], parts[1]).T * SCORE_SCALE
            d_query = d_query * cos_ref[rows] - turn(d_query) * sin_ref[rows]
            out_ref[rows, lanes] = d_query.astype(BF16)
    d_key = dk_ref[...]
    d_key = d_key + pltpu.roll(d_key, HEAD_DIM, 1)
    d_key = d_key * cos_ref[...] - turn(d_key) * sin_ref[...]
    d_value = dv_ref[...]
    d_value = d_value + pltpu.roll(d_value, HEAD_DIM, 1)
    out_ref[:, pairs * PAIR :] = jnp.where(
        left_lanes(d_key.shape), d_key, d_value
    ).astype(BF16)


def attend_back(saved, grad, cosine, sine, lengths):
    query, key, value, log_sums = saved
    slots, q_width = query.shape
    block = min(BLOCK, slots)
    full = pl.BlockSpec(memory_space=pltpu.VMEM)
    return pl.pallas_call(
        functools.partial(attend_back_kernel, block),
        out_shape=jax.ShapeDtypeStruct((slots, q_width + PAIR), BF16),
        in_specs=[pl.BlockSpec(memory_space=pltpu.SMEM)] + [full] * 7,
        out_specs=full,
        scratch_shapes=[pltpu.VMEM((slots, PAIR), F32)] * 2,
        compiler_params=pltpu.CompilerParams(vmem_limit_bytes=48 << 20),
        cost_estimate=pl.CostEstimate(
            flops=10 * slots * slots * q_width, bytes_accessed=12 * slots * q_width,
            transcendentals=slots * slots * q_width // HEAD_DIM,
        ),
    )(lengths, query, key, value, log_sums, grad, cosine, sine)


def flip(mask, size):
    return [(i, i ^ mask) for i in range(size)]


def send(value, mask):
    return lax.ppermute(value, "dp", flip(mask, lax.axis_size("dp")))


def other(first):
    return 3 - first


def gather_near(shard, first):
    if lax.axis_size("dp") != 4:
        return None
    return (send(shard, first), send(shard, other(first)))


def gather_far(near, first):
    return None if near is None else send(near[0], other(first))


def place(pieces, masks, axis):
    me = lax.axis_index("dp")
    whole = None
    for mask, piece in zip(masks, pieces):
        size = piece.shape[axis]
        if whole is None:
            shape = list(piece.shape)
            shape[axis] = 4 * size
            whole = jnp.zeros(shape, piece.dtype)
        whole = lax.dynamic_update_slice_in_dim(whole, piece, (me ^ mask) * size, axis)
    return whole


def gather_direct(shard, axis):
    if lax.axis_size("dp") != 4:
        return lax.all_gather(shard, "dp", axis=axis, tiled=True)
    return place((shard, send(shard, 1), send(shard, 2), send(shard, 3)), range(4), axis)


def dp_block(partial, mask, axis):
    place = lax.axis_index("dp") ^ mask
    if partial.ndim == 2:
        size = partial.shape[1] // 4
        return lax.dynamic_slice_in_dim(partial, place * size, size, 1)
    return lax.dynamic_index_in_dim(partial, place, axis, keepdims=False)


def gather_halves(shard, near):
    if lax.axis_size("dp") != 4:
        return None
    half = shard.shape[0] // 2
    if near is None:
        return tuple(send(part, mask) for mask in (1, 2) for part in (shard[:half], shard[half:]))
    return (send(near[0], 2), send(near[3], 1))


def join_halves(shard, near, far, axis):
    if near is None:
        return lax.all_gather(shard, "dp", axis=axis, tiled=True)
    pieces = (shard,) + tuple(
        jnp.concatenate(pair, axis=0) for pair in (near[:2], near[2:], far)
    )
    return place(pieces, range(4), axis)


def scatter_first(partial, axis, first):
    if lax.axis_size("dp") != 4:
        return lax.psum_scatter(
            partial.astype(BF16), "dp", scatter_dimension=axis, tiled=partial.ndim == 2
        )
    return tuple(send(dp_block(partial, mask, axis).astype(BF16), first) for mask in (3, first))


def scatter_second(partial, got, axis, first):
    if lax.axis_size("dp") != 4:
        return got.astype(F32)
    far, beside = got
    passed = dp_block(partial, other(first), axis).astype(F32) + far.astype(F32)
    last = send(passed.astype(BF16), other(first))
    own = dp_block(partial, 0, axis).astype(F32)
    return own + beside.astype(F32) + last.astype(F32)


def scatter_begin(partial, axis):
    if lax.axis_size("dp") != 4:
        return scatter_first(partial, axis, 1)
    return tuple(send(dp_block(partial, mask, axis).astype(BF16), mask) for mask in (1, 2, 3))


def scatter_end(partial, got, axis):
    if lax.axis_size("dp") != 4:
        return got.astype(F32)
    return sum((part.astype(F32) for part in got), dp_block(partial, 0, axis).astype(F32))


def scatter_direct(partial, axis):
    return scatter_end(partial, scatter_begin(partial, axis), axis)


def swap_dp(blocks):
    if lax.axis_size("dp") != 4:
        return exchange(blocks, "dp")
    parts = [dp_block(blocks, 0, 0)] + [send(dp_block(blocks, mask, 0), mask) for mask in (1, 2, 3)]
    return place([part[None] for part in parts], range(4), 0)


def exchange(blocks, axis_name):
    return lax.all_to_all(blocks, axis_name, split_axis=0, concat_axis=0, tiled=True)


def gather_seq(shard):
    return lax.all_gather(shard, "seq", axis=0, tiled=True)


def scatter_seq(partial):
    return lax.psum_scatter(
        partial.astype(BF16), "seq", scatter_dimension=0, tiled=True
    ).astype(F32)


def gate_up_kernel(me_ref, x_ref, *refs):
    pieces, (gate_ref, up_ref, *wholes, whole, sems, out_sems) = refs[:8], refs[8:]
    me = me_ref[0]
    sub, ff = pieces[0].shape[1:]
    copies = []
    for index, piece in enumerate(pieces):
        part, mask = divmod(index, 4)
        copies.append(
            pltpu.make_async_copy(piece, whole.at[part, :, me ^ mask], sems.at[index])
        )
    for copy in copies:
        copy.start()
    for copy in copies:
        copy.wait()
    writes = [
        pltpu.make_async_copy(whole.at[part], wholes[part], out_sems.at[part]) for part in range(2)
    ]
    for write in writes:
        write.start()
    depth = whole.shape[1] * whole.shape[2] * sub
    tile = min(512, ff)
    rows = min(256, x_ref.shape[0])

    @pl.loop(0, x_ref.shape[0] // rows)
    def _(step):
        span = pl.ds(pl.multiple_of(step * rows, rows), rows)
        for start in range(0, ff, tile):
            lanes = slice(start, start + tile)
            for part, out_ref in enumerate((gate_ref, up_ref)):
                out_ref[span, lanes] = dot(
                    x_ref[span, :], whole[part, :, :, :, lanes].reshape(depth, tile)
                )

    for write in writes:
        write.wait()


def gate_up_of(normed2, pieces):
    slots = normed2.shape[0]
    seqs, sub, ff = pieces[0].shape
    whole = (2, seqs, 4, sub, ff)
    full = pl.BlockSpec(memory_space=pltpu.VMEM)
    away = pl.BlockSpec(memory_space=pl.ANY)
    shape = jax.ShapeDtypeStruct
    me = lax.axis_index("dp").astype(jnp.int32).reshape(1)
    return pl.pallas_call(
        gate_up_kernel,
        out_shape=(shape((slots, ff), F32),) * 2 + (shape(whole[1:], BF16),) * 2,
        in_specs=[pl.BlockSpec(memory_space=pltpu.SMEM), full] + [away] * len(pieces),
        out_specs=(full, full, away, away),
        scratch_shapes=[
            pltpu.VMEM(whole, BF16),
            pltpu.SemaphoreType.DMA((len(pieces),)),
            pltpu.SemaphoreType.DMA((2,)),
        ],
        compiler_params=pltpu.CompilerParams(vmem_limit_bytes=56 << 20),
        cost_estimate=pl.CostEstimate(
            flops=2 * slots * normed2.shape[1] * 2 * ff,
            bytes_accessed=8 * slots * ff + 8 * ff * normed2.shape[1],
            transcendentals=0,
        ),
    )(me, normed2, *pieces)


def local(tokens, lengths, w_qkv, w_out, w_gate_up, w_down, gains, cotangent):
    tok_rows, width = tokens.shape[1:]
    seqs, ranks = lax.axis_size("seq"), lax.axis_size("dp")
    slots = tok_rows * seqs
    q_width = ATTN // seqs
    repeats = max(1, seqs // KV_HEADS)
    ff = FF // seqs
    sub = w_qkv.shape[0] // ranks

    first_slot = lax.axis_index("seq") * tok_rows
    length = lengths[0]
    valid_rows = ((first_slot + jnp.arange(tok_rows)) < length).astype(F32)[:, None]
    cosine, sine = rotary_pair(slots)

    def split_qkv(rows):
        def heads(block):
            block = block.reshape(sub, KV_HEADS, HEAD_DIM)
            return jnp.repeat(block, repeats, axis=1)

        query = rows[:, :ATTN].reshape(sub, seqs, q_width)
        joined = jnp.concatenate(
            [query, heads(rows[:, ATTN : ATTN + KV]), heads(rows[:, ATTN + KV :])], axis=2
        )
        return joined.transpose(1, 0, 2)

    def join_qkv(blocks):
        def heads(block):
            block = block.reshape(sub, KV_HEADS, repeats, HEAD_DIM)
            if repeats > 1:
                block = block.astype(F32).sum(axis=2).astype(BF16)
            return block.reshape(sub, KV)

        blocks = blocks.transpose(1, 0, 2)
        key_part = heads(blocks[:, :, q_width : q_width + HEAD_DIM])
        value_part = heads(blocks[:, :, q_width + HEAD_DIM :])
        return jnp.concatenate([blocks[:, :, :q_width].reshape(sub, ATTN), key_part, value_part], axis=1)

    all_tokens = gather_seq(tokens[0])
    qkv_rows = swap_dp(w_qkv.reshape(ranks, sub, -1)).transpose(1, 0, 2).reshape(sub, -1)
    per_block = w_gate_up.shape[1] // ff
    qkv_rows, w_gate_up = tie((qkv_rows, w_gate_up))
    gu_rows = swap_dp(
        w_gate_up.reshape(ranks, sub, per_block, ff).transpose(0, 2, 1, 3)
    ).reshape(2, seqs, sub, ff)
    def with_gains(blocks, pair):
        rows = jnp.pad(pair, ((0, 0), (0, 6), (0, blocks.shape[2] - pair.shape[2])))
        return jnp.concatenate([blocks, rows.astype(BF16)], axis=1)

    gain_rows = jnp.broadcast_to(gains.T, (seqs, 2, gains.shape[0]))
    qkv_got = exchange(with_gains(split_qkv(qkv_rows), gain_rows), "seq")
    qkv_got, gu_rows = tie((qkv_got, gu_rows))
    gu_mine = exchange(gu_rows.transpose(1, 0, 2, 3), "seq")
    qkv_mine = qkv_got[:, :sub]
    all_gains = qkv_got[:, sub : sub + 2, : gains.shape[0]].transpose(1, 0, 2)
    all_gains = all_gains.reshape(2, width).astype(F32)
    gain_first, gain_second = all_gains[0], all_gains[1]
    my_qkv = gather_direct(qkv_mine[:, None], 1).reshape(width, q_width + PAIR)
    all_tokens, my_qkv, w_out, w_down = tie((all_tokens, my_qkv, w_out, w_down))
    my_out = gather_direct(w_out, 1)
    down_near = gather_halves(w_down, None)

    x_all = all_tokens.astype(F32)
    inv_all = lax.rsqrt(jnp.mean(x_all * x_all, axis=1, keepdims=True) + EPSILON)
    normed = (x_all * inv_all * gain_first).astype(BF16)
    qkv = dot(normed, my_qkv)
    attended, *saved = attend(qkv, cosine, sine, lengths, q_width)
    attended, gu_mine, my_out, down_near = tie((attended, gu_mine, my_out, down_near))
    gate_mine, up_mine = gu_mine[:, 0], gu_mine[:, 1]
    gate_near, up_near = gather_near(gate_mine, 1), gather_near(up_mine, 2)

    x = tokens[0].astype(F32)
    branch = scatter_seq(dot(attended, my_out))
    branch, gate_near, up_near, down_near = tie((branch, gate_near, up_near, down_near))
    gate_far, up_far = gather_far(gate_near, 1), gather_far(up_near, 2)
    down_far = gather_halves(w_down, down_near)
    hidden = x + RESIDUAL_SCALE * branch
    inv_second = lax.rsqrt(jnp.mean(hidden * hidden, axis=1, keepdims=True) + EPSILON)
    unit_second = hidden * inv_second
    normed2 = gather_seq((unit_second * gain_second).astype(BF16))
    upstream = cotangent[0].astype(F32) * valid_rows
    normed2, gate_far, up_far, down_far, late_grad = tie(
        (normed2, gate_far, up_far, down_far, (RESIDUAL_SCALE * upstream).astype(BF16))
    )
    down_grad = gather_seq(late_grad)
    my_down = join_halves(w_down, down_near, down_far, 1)

    if gate_near is None:
        my_gate, my_up = (
            lax.all_gather(mine, "dp", axis=1).reshape(width, ff) for mine in (gate_mine, up_mine)
        )
        gate_vals, up_vals = dot(normed2, my_gate), dot(normed2, my_up)
    else:
        pieces = (gate_mine, *gate_near, gate_far, up_mine, up_near[1], up_near[0], up_far)
        gate_vals, up_vals, *wholes = gate_up_of(normed2, pieces)
        my_gate, my_up = (whole.reshape(width, ff) for whole in wholes)
    sigmoid_gate = jax.nn.sigmoid(gate_vals)
    mixed = (gate_vals * sigmoid_gate * up_vals).astype(BF16)
    down_sum = dot(mixed, my_down).astype(BF16)
    down_grad, down_sum = tie((down_grad, down_sum))
    down_out = scatter_seq(down_sum)
    down_partial = dot_tn(mixed, down_grad).astype(BF16)
    down_grad, down_partial = tie((down_grad, down_partial))
    down_got = scatter_begin(down_partial, 1)
    mixed_grad = dot_nt(down_grad, my_down)
    gate_grad = (
        mixed_grad * up_vals * sigmoid_gate * (1.0 + gate_vals * (1.0 - sigmoid_gate))
    ).astype(BF16)
    up_grad = (mixed_grad * gate_vals * sigmoid_gate).astype(BF16)
    normed2_sum = (dot_nt(gate_grad, my_gate) + dot_nt(up_grad, my_up)).astype(BF16)

    gate_partial = dot_tn(normed2, gate_grad).astype(BF16).reshape(seqs, ranks, sub, ff)
    up_partial = dot_tn(normed2, up_grad).astype(BF16).reshape(seqs, ranks, sub, ff)
    normed2_sum, down_out, gate_partial, up_partial, down_got = tie(
        (normed2_sum, down_out, gate_partial, up_partial, down_got)
    )
    normed2_grad = scatter_seq(normed2_sum)
    gate_got = scatter_first(gate_partial, 1, 1)
    up_got = scatter_first(up_partial, 1, 2)
    normed2_grad, gate_got, up_got = tie((normed2_grad, gate_got, up_got))

    unit_grad2 = normed2_grad * gain_second
    hidden_grad = upstream + inv_second * (
        unit_grad2 - unit_second * jnp.mean(unit_grad2 * unit_second, axis=1, keepdims=True)
    )
    gain_second_term = jnp.sum(normed2_grad * unit_second, axis=0)
    branch_grad = gather_seq((RESIDUAL_SCALE * hidden_grad).astype(BF16))
    gu_summed = jnp.stack(
        [
            scatter_second(gate_partial, gate_got, 1, 1).astype(BF16),
            scatter_second(up_partial, up_got, 1, 2).astype(BF16),
        ],
        axis=1,
    )
    gu_summed, down_partial = tie((gu_summed, down_partial))
    branch_grad, gu_summed = tie((branch_grad, gu_summed))
    gu_blocks = exchange(gu_summed, "seq")

    attended_grad = dot_nt(branch_grad, my_out).astype(BF16)
    qkv_grad = attend_back(saved, attended_grad, cosine, sine, lengths)
    qkv_grad, down_partial = tie((qkv_grad, down_partial))
    grad_down = scatter_end(down_partial, down_got, 1)
    normed_partial = dot_nt(qkv_grad, my_qkv)
    qkv_partial = dot_tn(normed, qkv_grad).astype(BF16).reshape(seqs, ranks, sub, -1)
    qkv_summed = scatter_direct(qkv_partial, 1).astype(BF16)
    out_partial = dot_tn(attended, branch_grad).astype(BF16)
    unit_all = x_all * inv_all
    gain_first_term = jnp.sum(normed_partial * unit_all, axis=0)
    gains_term = jnp.stack([gain_first_term, gain_second_term]).reshape(2, seqs, -1)
    qkv_blocks = with_gains(qkv_summed, gains_term.transpose(1, 0, 2))
    grad_out = scatter_direct(out_partial, 1)
    normed_sum, gu_blocks, grad_down, qkv_blocks, grad_out = tie(
        (normed_partial.astype(BF16), gu_blocks, grad_down, qkv_blocks, grad_out)
    )
    normed_grad = scatter_seq(normed_sum)
    gu_back = swap_dp(
        gu_blocks.transpose(1, 0, 2, 3).reshape(ranks, per_block, sub, ff)
    )
    qkv_back, gu_back = tie((exchange(qkv_blocks, "seq"), gu_back))
    gain_blocks = qkv_back[:, sub : sub + 2, : gains.shape[0]]
    qkv_back = join_qkv(qkv_back[:, :sub])
    grad_qkv = (
        swap_dp(qkv_back.reshape(sub, ranks, -1).transpose(1, 0, 2))
        .reshape(w_qkv.shape)
        .astype(F32)
    )
    grad_gate_up = gu_back.transpose(0, 2, 1, 3).reshape(w_gate_up.shape).astype(F32)

    grad_gains = jnp.sum(gain_blocks.astype(F32), axis=0)
    if ranks == 4:
        grad_gains = grad_gains + send(grad_gains, 1)
        grad_gains = (grad_gains + send(grad_gains, 2)).T
    else:
        grad_gains = lax.psum(grad_gains, "dp").T

    normed_grad, grad_qkv, grad_out, grad_gate_up, grad_gains = tie(
        (normed_grad, grad_qkv, grad_out, grad_gate_up, grad_gains)
    )
    output = (valid_rows * (hidden + RESIDUAL_SCALE * down_out)).astype(BF16)
    inv_first = lax.rsqrt(jnp.mean(x * x, axis=1, keepdims=True) + EPSILON)
    unit_first = x * inv_first
    unit_grad1 = normed_grad * gain_first
    token_grad = hidden_grad + inv_first * (
        unit_grad1 - unit_first * jnp.mean(unit_grad1 * unit_first, axis=1, keepdims=True)
    )
    return (output[None], token_grad[None], grad_qkv, grad_out, grad_gate_up, grad_down, grad_gains)


def solution(mesh):
    in_specs = (
        P("dp", "seq", None),
        P("dp"),
        P("seq", "dp"),
        P("seq", "dp"),
        P("seq", "dp"),
        P("seq", "dp"),
        P("seq", None),
        P("dp", "seq", None),
    )
    out_specs = (
        P("dp", "seq", None),
        P("dp", "seq", None),
        P("seq", "dp"),
        P("seq", "dp"),
        P("seq", "dp"),
        P("seq", "dp"),
        P("seq", None),
    )
    return jax.shard_map(local, mesh=mesh, in_specs=in_specs, out_specs=out_specs, check_vma=False)
```
